512 devices in a mesh: ctx: 16 (over z, core), head: 32 (over x, y).
Axes of the slice: x: 4, y: 8, z: 8, core: 2. Of those that a mesh axis runs over, the one named last changes fastest.
Arguments:
- x_in: bfloat16 [4096, 16384], P(('ctx', 'head')), may hold values from -6 to 6
- grad_y: bfloat16 [4096, 16384], P(('ctx', 'head')), may hold values from -6 to 6
- b_in: bfloat16 [4096, 2048], P(('ctx', 'head')), may hold values from -0.29882812 to 0.29882812
- c_in: bfloat16 [4096, 2048], P(('ctx', 'head')), may hold values from -0.375 to 0.375
- dt: bfloat16 [4096, 256], P(('ctx', 'head')), may hold values from 0.25 to 2
- conv_weight: float32 [4, 16384], P(None, 'head'), may hold values from -3 to 3
- conv_bias: float32 [16384], P('head'), may hold values from -3 to 3
- decay_rate: float32 [256], P('head'), may hold values from 1e-05 to 0.02
- skip: float32 [256], P('head'), may hold values from 0.5 to 1.5
Outputs:
- grad_x: bfloat16 [4096, 16384], P(('ctx', 'head'))
- grad_b: bfloat16 [4096, 2048], P(('ctx', 'head'))
- grad_c: bfloat16 [4096, 2048], P(('ctx', 'head'))
- grad_dt: float32 [4096, 256], P(('ctx', 'head'))
The draws below stay inside these ranges and needn't reach their ends.
All inputs are finite; a program needn't handle non-finite values.
Results may differ from the reference program's by a relative error of at most 0.001.
Values may be sent and summed in bfloat16 or wider, within the bound.
A program may use at most 64 MiB of HBM per device.

```python
import math
import jax
import jax.numpy as jnp
from jax import lax

HEADS = 256
HEAD_DIM = 64
STATE = 256
GROUPS = 8
CONV = 4
TOKENS = 4096


def levels(rng, shape, split, low, high):
    def one(dim, parts):
        heights = jax.random.uniform(jax.random.fold_in(jax.random.fold_in(rng, 6), dim), (parts,), jnp.float32, low / len(split), high / len(split))
        return jnp.repeat(jnp.exp(heights), shape[dim] // parts).reshape((-1,) + (1,) * (len(shape) - dim - 1))

    gain = one(*split[0])
    for cut in split[1:]:
        gain = gain * one(*cut)
    return gain


def gaussian(stream_key, dims, scale, reach, cuts=(), held_as=jnp.bfloat16):
    entries = scale * jax.random.normal(stream_key, dims, jnp.float32)
    if cuts:
        entries = entries * levels(stream_key, dims, cuts, -0.22, 0.18)
    return jnp.clip(entries, -reach, reach).astype(held_as)


def setup_inputs(seed: int = 0) -> dict:
    seeds = jax.random.split(jax.random.key(seed), 10)
    return {
        "x_in": gaussian(seeds[0], (TOKENS, HEADS * HEAD_DIM), 1.0, 6.0, ((0, 512),)),
        "grad_y": gaussian(seeds[1], (TOKENS, HEADS * HEAD_DIM), 1.0, 6.0, ((0, 512),)),
        "b_in": gaussian(seeds[2], (TOKENS, GROUPS * STATE), 0.05, 0.29882812, ((0, 512),)),
        "c_in": gaussian(seeds[3], (TOKENS, GROUPS * STATE), STATE ** -0.5, 0.375, ((0, 512),)),
        "dt": jnp.clip(jnp.exp(math.log(2.0) - 2.0794415 * jax.random.uniform(seeds[4], (TOKENS, HEADS), jnp.float32) ** levels(seeds[4], (TOKENS, HEADS), ((0, 512),), -0.2, 0.2)), 0.25, 2.0).astype(jnp.bfloat16),
        "conv_weight": gaussian(seeds[5], (CONV, HEADS * HEAD_DIM), CONV ** -0.5, 3.0, ((1, 32),), jnp.float32),
        "conv_bias": gaussian(seeds[6], (HEADS * HEAD_DIM,), 0.5, 3.0, ((0, 32),), jnp.float32),
        "decay_rate": jnp.clip(jnp.exp(math.log(0.02) - 7.6009025 * jax.random.uniform(seeds[7], (HEADS,), jnp.float32) ** levels(seeds[7], (HEADS,), ((0, 32),), -0.2, 0.2)), 9.999999747378752e-06, 0.02),
        "skip": jnp.clip(0.5 + 1.0 * jax.random.uniform(seeds[8], (HEADS,), jnp.float32) ** levels(seeds[8], (HEADS,), ((0, 32),), -0.2, 0.2), 0.5, 1.5),
    }


HIGH = lax.Precision.HIGHEST

def conv_silu(padded, weight, bias):
    length = padded.shape[0] - CONV + 1
    summed = bias[None, :] + weight[0][None, :] * padded[0:length]
    for k in range(1, CONV):
        summed = summed + weight[k][None, :] * padded[k:k + length]
    return jax.nn.silu(summed)

def block_terms(carried, x_block, dt_block, b_block, c_block, head_rate):
    width = x_block.shape[0]
    cumul = jnp.cumsum(-dt_block * head_rate[None, :], axis=0)
    causal = (lax.broadcasted_iota(jnp.int32, (width, width), 0) >= lax.broadcasted_iota(jnp.int32, (width, width), 1))[:, :, None]
    gaps = cumul[:, None, :] - cumul[None, :, :]
    decay_mat = jnp.where(causal, jnp.exp(jnp.where(causal, gaps, 0.0)), 0.0)
    gram_mat = jnp.dot(c_block, b_block.T, precision=HIGH)
    mixing = decay_mat * gram_mat[:, :, None] * dt_block[None, :, :]
    output = jnp.einsum('tsh,shp->thp', mixing, x_block, precision=HIGH)
    output = output + jnp.exp(cumul)[:, :, None] * jnp.einsum('tn,hpn->thp', c_block, carried, precision=HIGH)
    tail_wt = jnp.exp(cumul[-1][None, :] - cumul) * dt_block
    carried = jnp.exp(cumul[-1])[:, None, None] * carried + jnp.einsum('shp,sn->hpn', x_block * tail_wt[:, :, None], b_block, precision=HIGH)
    return (carried, output)

def group_forward(x_group, dt_group, b_group, c_group, weight, bias, head_rate, skip_head):
    length = x_group.shape[0]
    head_count = head_rate.shape[0]
    padded = jnp.pad(x_group, ((CONV - 1, 0), (0, 0)))
    activ = conv_silu(padded, weight, bias).reshape(length, head_count, HEAD_DIM)
    width = math.gcd(length, 128)
    count = length // width
    pieces = (activ.reshape(count, width, head_count, HEAD_DIM), dt_group.reshape(count, width, head_count), b_group.reshape(count, width, STATE), c_group.reshape(count, width, STATE))

    def advance(carried, piece):
        return block_terms(carried, piece[0], piece[1], piece[2], piece[3], head_rate)
    start = jnp.zeros((head_count, HEAD_DIM, STATE), jnp.float32)
    _, outputs = lax.scan(advance, start, pieces)
    outputs = outputs.reshape(length, head_count, HEAD_DIM) + skip_head[None, :, None] * activ
    return outputs.reshape(length, head_count * HEAD_DIM)

def reference(x_in, grad_y, b_in, c_in, dt, conv_weight, conv_bias, decay_rate, skip):
    per_heads = HEADS // GROUPS
    chans = per_heads * HEAD_DIM

    def one_group(index):
        x_group = lax.dynamic_slice_in_dim(x_in, index * chans, chans, 1).astype(jnp.float32)
        dy_group = lax.dynamic_slice_in_dim(grad_y, index * chans, chans, 1).astype(jnp.float32)
        b_group = lax.dynamic_slice_in_dim(b_in, index * STATE, STATE, 1).astype(jnp.float32)
        c_group = lax.dynamic_slice_in_dim(c_in, index * STATE, STATE, 1).astype(jnp.float32)
        dt_group = lax.dynamic_slice_in_dim(dt, index * per_heads, per_heads, 1).astype(jnp.float32)
        weight = lax.dynamic_slice_in_dim(conv_weight, index * chans, chans, 1)
        bias = lax.dynamic_slice_in_dim(conv_bias, index * chans, chans, 0)
        head_rate = lax.dynamic_slice_in_dim(decay_rate, index * per_heads, per_heads, 0)
        skip_head = lax.dynamic_slice_in_dim(skip, index * per_heads, per_heads, 0)

        def forward_fn(x_arg, dt_arg, b_arg, c_arg):
            return group_forward(x_arg, dt_arg, b_arg, c_arg, weight, bias, head_rate, skip_head)
        _, pullback = jax.vjp(forward_fn, x_group, dt_group, b_group, c_group)
        return pullback(dy_group)
    g_x, g_dt, g_b, g_c = lax.map(one_group, jnp.arange(GROUPS, dtype=jnp.int32))
    g_x = jnp.moveaxis(g_x, 0, 1).reshape(TOKENS, HEADS * HEAD_DIM)
    g_dt = jnp.moveaxis(g_dt, 0, 1).reshape(TOKENS, HEADS)
    g_b = jnp.moveaxis(g_b, 0, 1).reshape(TOKENS, GROUPS * STATE)
    g_c = jnp.moveaxis(g_c, 0, 1).reshape(TOKENS, GROUPS * STATE)
    return (g_x.astype(jnp.bfloat16), g_b.astype(jnp.bfloat16), g_c.astype(jnp.bfloat16), g_dt)
```

```python
import functools

import jax
import jax.numpy as jnp
from jax import lax
from jax.experimental import pallas as pl
from jax.experimental.pallas import tpu as pltpu
from jax.sharding import PartitionSpec as P

HEAD_DIM = 64
STATE = 256
GROUPS = 8
CONV = 4
LANES = 128
F32 = jnp.float32
BF16 = jnp.bfloat16


def nn(a, b):
    return lax.dot_general(a, b, (((1,), (0,)), ((), ())), preferred_element_type=F32)


def nt(a, b):
    return lax.dot_general(a, b, (((1,), (1,)), ((), ())), preferred_element_type=F32)


def split(value, pieces=2):
    parts = []
    for _ in range(pieces):
        part = value.astype(BF16)
        parts.append(part)
        value = value - part.astype(F32)
    return parts


def exact_by(dot, exact, wide):
    hi, lo = split(wide)
    return dot(exact, hi) + dot(exact, lo)


def wide_by(dot, wide, exact):
    hi, lo = split(wide)
    return dot(hi, exact) + dot(lo, exact)


def three(dot, left, right):
    lh, ll = split(left)
    rh, rl = split(right)
    return dot(lh, rh) + (dot(lh, rl) + dot(ll, rh))


def expand(cols, width):
    lane = lax.broadcasted_iota(jnp.int32, (cols.shape[0], LANES), 1)
    parts = [
        jnp.where(lane < HEAD_DIM, cols[:, h : h + 1], cols[:, h + 1 : h + 2])
        for h in range(0, width // HEAD_DIM, 2)
    ]
    return jnp.concatenate(parts, axis=1)


def segments(value):
    width = value.shape[1]
    row = lax.broadcasted_iota(jnp.int32, (width, LANES), 0)
    col = lax.broadcasted_iota(jnp.int32, (width, LANES), 1)
    pick = jnp.where(
        (row >= col * HEAD_DIM) & (row < (col + 1) * HEAD_DIM), 1.0, 0.0
    ).astype(BF16)
    return wide_by(nn, value, pick)


def triangle(length, lower):
    row = lax.broadcasted_iota(jnp.int32, (length, length), 0)
    col = lax.broadcasted_iota(jnp.int32, (length, length), 1)
    return row >= col if lower else row <= col


def columns(width):
    x_to = width
    dy_to = 2 * width
    b_to = dy_to + STATE
    c_to = b_to + STATE
    return x_to, dy_to, b_to, c_to


def convolve(rows_ref, edge_ref, par_ref, ext):
    length, width = rows_ref.shape[0], edge_ref.shape[1]
    ext[0:8, :] = edge_ref[...].astype(F32)
    ext[8 : 8 + length, :] = rows_ref[:, 0:width].astype(F32)
    conv = par_ref[4:5, :] + par_ref[0:1, :] * ext[5 : 5 + length, :]
    for k in range(1, CONV):
        conv = conv + par_ref[k : k + 1, :] * ext[5 + k : 5 + k + length, :]
    return conv, 1.0 / (1.0 + jnp.exp(-conv))


def decays(rows_ref, par_ref, width):
    length = rows_ref.shape[0]
    c_to = columns(width)[3]
    dt16 = rows_ref[:, c_to : c_to + LANES]
    lower = jnp.where(triangle(length, True), 1.0, 0.0).astype(BF16)
    rate = par_ref[6:7, 0:LANES]
    return dt16.astype(F32), rate, -rate * nn(lower, dt16)


def states_kernel(parts, rows_ref, edge_ref, par_ref, out_ref, ext):
    length, width = rows_ref.shape[0], edge_ref.shape[1]
    x_to, dy_to, b_to, c_to = columns(width)
    conv, sig = convolve(rows_ref, edge_ref, par_ref, ext)
    activ = conv * sig
    dt, rate, cumul = decays(rows_ref, par_ref, width)
    tail_wt = jnp.exp(cumul[length - 1 : length, :] - cumul) * dt
    grow = expand(jnp.exp(cumul), width)
    b_turned = rows_ref[:, dy_to:b_to].astype(F32).T.astype(BF16)
    c_turned = rows_ref[:, b_to:c_to].astype(F32).T.astype(BF16)
    state = exact_by(nn, b_turned, activ * expand(tail_wt, width))
    pull = exact_by(nn, c_turned, rows_ref[:, x_to:dy_to].astype(F32) * grow)
    piece = STATE // parts
    last = jnp.broadcast_to(grow[length - 1 : length, :], (8, width))
    for j in range(parts):
        out_ref[j, 0:piece, :] = state[j * piece : (j + 1) * piece, :]
        out_ref[j, piece : 2 * piece, :] = pull[j * piece : (j + 1) * piece, :]
        out_ref[j, 2 * piece : 2 * piece + 8, :] = last


def scan_kernel(in_ref, out_ref):
    parts = in_ref.shape[0]
    piece = out_ref.shape[1] // 2
    state = jnp.zeros((piece, in_ref.shape[2]), F32)
    for j in range(parts):
        out_ref[j, 0:piece, :] = state
        state = in_ref[j, 2 * piece : 2 * piece + 1, :] * state + in_ref[j, 0:piece, :]
    state = jnp.zeros((piece, in_ref.shape[2]), F32)
    for j in range(parts - 1, -1, -1):
        out_ref[j, piece : 2 * piece, :] = state
        state = (
            in_ref[j, 2 * piece : 2 * piece + 1, :] * state
            + in_ref[j, piece : 2 * piece, :]
        )


def main_kernel(rows_ref, edge_ref, par_ref, st_ref, out_ref, ends_ref, ext):
    length, width = rows_ref.shape[0], edge_ref.shape[1]
    x_to, dy_to, b_to, c_to = columns(width)
    parts = st_ref.shape[0]
    piece = STATE // parts
    conv, sig = convolve(rows_ref, edge_ref, par_ref, ext)
    activ = conv * sig
    slope = sig * (1.0 + conv * (1.0 - sig))
    dt, rate, cumul = decays(rows_ref, par_ref, width)
    grow = expand(jnp.exp(cumul), width)
    tail = expand(jnp.exp(cumul[length - 1 : length, :] - cumul), width)
    dt_wide = expand(dt, width)
    turned = cumul.T
    dy16 = rows_ref[:, x_to:dy_to]
    dy = dy16.astype(F32)
    b16 = rows_ref[:, dy_to:b_to]
    c16 = rows_ref[:, b_to:c_to]
    state = jnp.concatenate([st_ref[j, 0:piece, :] for j in range(parts)], axis=0)
    pull = jnp.concatenate([st_ref[j, piece : 2 * piece, :] for j in range(parts)], axis=0)
    source = activ * dt_wide

    gram = nt(c16, b16)
    gram_turned = nt(b16, c16)
    lower = triangle(length, True)
    upper = triangle(length, False)
    lane = lax.broadcasted_iota(jnp.int32, (length, LANES), 1)
    g_gram = jnp.zeros((length, length), F32)
    g_cumul = jnp.zeros((length, LANES), F32)
    inner = []
    for pair in range(width // LANES):
        at = slice(pair * LANES, (pair + 1) * LANES)
        src_hi, src_lo = split(source[:, at])
        halves = []
        for side in range(2):
            h = 2 * pair + side
            own = lane < HEAD_DIM if side == 0 else lane >= HEAD_DIM
            dy_own = jnp.where(own, dy[:, at], 0.0).astype(BF16)
            col = cumul[:, h : h + 1]
            row = turned[h : h + 1, :]
            decay = jnp.where(lower, jnp.exp(jnp.minimum(col - row, 0.0)), 0.0)
            inside = decay * (nt(dy_own, src_hi) + nt(dy_own, src_lo))
            g_gram = g_gram + inside
            g_cumul = g_cumul + jnp.where(
                lane == h, jnp.sum(inside * gram, axis=1, keepdims=True), 0.0
            )
            mixing = gram_turned * jnp.where(
                upper, jnp.exp(jnp.minimum(row - col, 0.0)), 0.0
            )
            halves.append(wide_by(nn, mixing, dy16[:, at]))
        inner.append(jnp.where(lane < HEAD_DIM, halves[0], halves[1]))
    pulled = tail * exact_by(nn, b16, pull)
    g_source = jnp.concatenate(inner, axis=1) + pulled

    dy_grown = dy * grow
    direct = segments(activ * g_source)
    g_cumul = g_cumul + segments(dy_grown * exact_by(nn, c16, state)) - dt * direct
    carried = jnp.sum(source * pulled, axis=0, keepdims=True) + grow[
        length - 1 : length, :
    ] * jnp.sum(state * pull, axis=0, keepdims=True)
    carried = segments(jnp.broadcast_to(carried, (16, width)))[0:1, :]
    after = jnp.where(upper, 1.0, 0.0).astype(BF16)
    pieces = split(g_cumul, 3)
    later = nn(after, pieces[0]) + (nn(after, pieces[1]) + nn(after, pieces[2]))
    g_dt = direct - rate * (later + carried)

    g_c = wide_by(nn, g_gram, b16) + three(nt, dy_grown, state)
    g_b = wide_by(nn, g_gram.T, c16) + three(nt, source * tail, pull)

    g_conv = (dt_wide * g_source + expand(par_ref[7:8, 0:LANES], width) * dy) * slope
    ext[0:length, :] = g_conv
    ext[length : length + 8, :] = jnp.zeros((8, width), F32)
    g_x = par_ref[3:4, :] * g_conv
    for k in range(CONV - 1):
        g_x = g_x + par_ref[k : k + 1, :] * ext[CONV - 1 - k : CONV - 1 - k + length, :]
    out_ref[:, 0:width] = g_x.astype(BF16)
    ends_ref[0:8, :] = g_conv[0:8, :]
    ends_ref[8:16, :] = g_x[length - 8 : length, :]
    at = width
    for value in (g_b, g_c):
        for part in split(value):
            out_ref[:, at : at + STATE] = part
            at += STATE
    merged = jnp.zeros((length, LANES), F32)
    for j, part in enumerate(split(g_dt, 3)):
        part = part.astype(F32)
        merged = merged + (pltpu.roll(part, j * (width // HEAD_DIM), 1) if j else part)
    out_ref[:, at : at + LANES] = merged.astype(BF16)


def call(kernel, shapes, scratch, *operands):
    return pl.pallas_call(
        kernel,
        out_shape=shapes,
        in_specs=[pl.BlockSpec(memory_space=pltpu.VMEM)] * len(operands),
        out_specs=jax.tree.map(lambda _: pl.BlockSpec(memory_space=pltpu.VMEM), shapes),
        scratch_shapes=scratch,
        compiler_params=pltpu.CompilerParams(vmem_limit_bytes=56 * 1024 * 1024),
    )(*operands)


def passed_along(value, axis, by):
    count = lax.axis_size(axis)
    pairs = [(i, i + by) for i in range(count) if 0 <= i + by < count]
    return lax.ppermute(value, axis, pairs)


def shards(x_in, grad_y, b_in, c_in, dt, conv_weight, conv_bias, decay_rate, skip):
    n_head = lax.axis_size("head")
    n_ctx = lax.axis_size("ctx")
    per_group = n_head // GROUPS
    tok_dev = x_in.shape[0]
    heads_dev = decay_rate.shape[0]
    width = heads_dev * HEAD_DIM
    length = tok_dev * n_head

    def spread(value):
        value = value.reshape(tok_dev, GROUPS, 1, STATE)
        value = jnp.broadcast_to(value, (tok_dev, GROUPS, per_group, STATE))
        return value.reshape(tok_dev, n_head, STATE)

    sent = jnp.concatenate(
        [
            x_in.reshape(tok_dev, n_head, width),
            grad_y.reshape(tok_dev, n_head, width),
            spread(b_in),
            spread(c_in),
            jnp.pad(
                dt.reshape(tok_dev, n_head, heads_dev),
                ((0, 0), (0, 0), (0, LANES - heads_dev)),
            ),
        ],
        axis=2,
    )
    total = sent.shape[2]
    rows = lax.all_to_all(
        sent.transpose(1, 0, 2), "head", split_axis=0, concat_axis=0, tiled=True
    ).reshape(length, total)
    edge = passed_along(rows[length - 8 :, :width], "ctx", 1)
    wide = lambda value: jnp.pad(value[None, :], ((0, 0), (0, width - heads_dev)))
    params = jnp.concatenate(
        [conv_weight, conv_bias[None, :], conv_bias[None, :], wide(decay_rate), wide(skip)], axis=0
    )
    ext = [pltpu.VMEM((length + 8, width), F32)]
    piece = STATE // n_ctx
    local = call(
        functools.partial(states_kernel, n_ctx),
        jax.ShapeDtypeStruct((n_ctx, 2 * piece + 8, width), F32),
        ext,
        rows,
        edge,
        params,
    )
    local = lax.all_to_all(local, "ctx", split_axis=0, concat_axis=0, tiled=True)
    scanned = call(
        scan_kernel, jax.ShapeDtypeStruct((n_ctx, 2 * piece, width), F32), [], local
    )
    states = lax.all_to_all(scanned, "ctx", split_axis=0, concat_axis=0, tiled=True)
    outs, ends = call(
        main_kernel,
        (
            jax.ShapeDtypeStruct((length, width + 4 * STATE + LANES), BF16),
            jax.ShapeDtypeStruct((16, width), F32),
        ),
        ext,
        rows,
        edge,
        params,
        states,
    )
    first = passed_along(ends[0:8], "ctx", -1)
    tail = ends[8:16]
    for k in range(CONV - 1):
        count = CONV - 1 - k
        tail = tail + jnp.pad(
            conv_weight[k][None, :] * first[0:count], ((8 - count, 0), (0, 0))
        )
    outs = lax.dynamic_update_slice(outs, tail.astype(BF16), (length - 8, 0))
    back = lax.all_to_all(
        outs.reshape(n_head, tok_dev, outs.shape[1]),
        "head",
        split_axis=0,
        concat_axis=0,
        tiled=True,
    )
    grad_x = back[:, :, :width].transpose(1, 0, 2).reshape(tok_dev, n_head * width)

    def gathered(at):
        part = back[:, :, at : at + STATE].astype(F32) + back[
            :, :, at + STATE : at + 2 * STATE
        ].astype(F32)
        part = part.reshape(GROUPS, per_group, tok_dev, STATE).sum(axis=1)
        return part.transpose(1, 0, 2).reshape(tok_dev, GROUPS * STATE).astype(BF16)

    at = width + 4 * STATE
    g_dt = back[:, :, at : at + 3 * heads_dev].astype(F32)
    g_dt = g_dt.reshape(n_head, tok_dev, 3, heads_dev).sum(axis=2)
    grad_dt = g_dt.transpose(1, 0, 2).reshape(tok_dev, n_head * heads_dev)
    return (grad_x, gathered(width), gathered(width + 2 * STATE), grad_dt)


def solution(mesh):
    token = P(("ctx", "head"), None)
    in_specs = (token,) * 5 + (P(None, "head"), P("head"), P("head"), P("head"))
    return jax.shard_map(
        shards, mesh=mesh, in_specs=in_specs, out_specs=(token,) * 4, check_vma=False
    )
```

```python
import functools

import jax
import jax.numpy as jnp
from jax import lax
from jax.experimental import pallas as pl
from jax.experimental.pallas import tpu as pltpu
from jax.sharding import PartitionSpec as P

HEAD_DIM = 64
STATE = 256
GROUPS = 8
CONV = 4
LANES = 128
F32 = jnp.float32
BF16 = jnp.bfloat16
MESH = pl.DeviceIdType.MESH
CHUNK = 16


def nn(a, b):
    return lax.dot_general(a, b, (((1,), (0,)), ((), ())), preferred_element_type=F32)


def nt(a, b):
    return lax.dot_general(a, b, (((1,), (1,)), ((), ())), preferred_element_type=F32)


def split(value, pieces=2):
    parts = []
    for _ in range(pieces):
        part = value.astype(BF16)
        parts.append(part)
        value = value - part.astype(F32)
    return parts


def exact_by(dot, exact, wide):
    hi, lo = split(wide)
    return dot(exact, hi) + dot(exact, lo)


def wide_by(dot, wide, exact):
    hi, lo = split(wide)
    return dot(hi, exact) + dot(lo, exact)


def three(dot, left, right):
    lh, ll = split(left)
    rh, rl = split(right)
    return dot(lh, rh) + (dot(lh, rl) + dot(ll, rh))


def expand(cols, width):
    lane = lax.broadcasted_iota(jnp.int32, (cols.shape[0], LANES), 1)
    parts = [
        jnp.where(lane < HEAD_DIM, cols[:, h : h + 1], cols[:, h + 1 : h + 2])
        for h in range(0, width // HEAD_DIM, 2)
    ]
    return jnp.concatenate(parts, axis=1)


def segments(value):
    width = value.shape[1]
    row = lax.broadcasted_iota(jnp.int32, (width, LANES), 0)
    col = lax.broadcasted_iota(jnp.int32, (width, LANES), 1)
    pick = jnp.where(
        (row >= col * HEAD_DIM) & (row < (col + 1) * HEAD_DIM), 1.0, 0.0
    ).astype(BF16)
    return wide_by(nn, value, pick)


def triangle(length, lower):
    row = lax.broadcasted_iota(jnp.int32, (length, length), 0)
    col = lax.broadcasted_iota(jnp.int32, (length, length), 1)
    return row >= col if lower else row <= col


def columns(width):
    x_to = width
    dy_to = 2 * width
    b_to = dy_to + STATE
    c_to = b_to + STATE
    return x_to, dy_to, b_to, c_to


def convolve(rows_ref, par_ref, ext, width):
    length = rows_ref.shape[0]
    ext[8 : 8 + length, :] = rows_ref[:, 0:width].astype(F32)
    conv = par_ref[4:5, :] + par_ref[0:1, :] * ext[5 : 5 + length, :]
    for k in range(1, CONV):
        conv = conv + par_ref[k : k + 1, :] * ext[5 + k : 5 + k + length, :]
    return conv, 1.0 / (1.0 + jnp.exp(-conv))


def decays(rows_ref, par_ref, width):
    length = rows_ref.shape[0]
    c_to = columns(width)[3]
    dt16 = rows_ref[:, c_to : c_to + LANES]
    lower = jnp.where(triangle(length, True), 1.0, 0.0).astype(BF16)
    rate = par_ref[6:7, 0:LANES]
    return dt16.astype(F32), rate, -rate * nn(lower, dt16)


def block_kernel(
    n_ctx,
    rows_ref,
    par_ref,
    out_ref,
    ext,
    edge,
    top_out,
    top_in,
    mine,
    other,
    sib_local,
    decay_own,
    decay_sib,
    chain_in,
    chain_out,
    sib_out,
    sib_in,
    gram_sum,
    cumul_sum,
    inner,
    edge_sems,
    top_sems,
    local_sems,
    decay_sems,
    chain_send,
    chain_recv,
    sib_send,
    sib_recv,
):
    length, width = ext.shape[0] - 8, ext.shape[1]
    x_to, dy_to, b_to, c_to = columns(width)
    me = lax.axis_index("ctx")
    core = lax.rem(me, 2)
    chip = lax.div(me, 2)
    chips = n_ctx // 2
    sign = 1 - 2 * core
    place = core * (chips - 1) + sign * chip
    sibling = me + sign
    ahead = lax.rem(me + 2 * sign + n_ctx, n_ctx)
    following = lax.rem(me + 1, n_ctx)
    leading = lax.rem(me + n_ctx - 1, n_ctx)

    def remote(src, dst, sems, device):
        return pltpu.make_async_remote_copy(
            src_ref=src,
            dst_ref=dst,
            send_sem=sems[0],
            recv_sem=sems[1],
            device_id={"ctx": device},
            device_id_type=MESH,
        )

    barrier = pltpu.get_barrier_semaphore()
    for by in (1, 2, n_ctx - 2, n_ctx - 1):
        pl.semaphore_signal(
            barrier,
            inc=1,
            device_id={"ctx": lax.rem(me + by, n_ctx)},
            device_id_type=MESH,
        )
    pl.semaphore_wait(barrier, 4)

    edge_copy = remote(
        rows_ref.at[length - 16 : length, 0:width],
        edge,
        (edge_sems.at[0], edge_sems.at[1]),
        following,
    )
    edge_copy.start()

    dt, rate, cumul = decays(rows_ref, par_ref, width)
    grow = expand(jnp.exp(cumul), width)
    tail = expand(jnp.exp(cumul[length - 1 : length, :] - cumul), width)
    dt_wide = expand(dt, width)
    dy16 = rows_ref[:, x_to:dy_to]
    dy = dy16.astype(F32)
    b16 = rows_ref[:, dy_to:b_to]
    c16 = rows_ref[:, b_to:c_to]
    b_turned = b16.astype(F32).T.astype(BF16)
    c_turned = c16.astype(F32).T.astype(BF16)
    decay_own[...] = jnp.broadcast_to(grow[length - 1 : length, :], (8, width))
    decay_copy = remote(
        decay_own, decay_sib, (decay_sems.at[0], decay_sems.at[1]), sibling
    )
    decay_copy.start()
    dy_grown = dy * grow
    pull = exact_by(nn, c_turned, dy_grown)

    edge_copy.wait()
    ext[0:8, :] = jnp.where(me > 0, edge[...].astype(F32)[8:16, :], 0.0)
    conv, sig = convolve(rows_ref, par_ref, ext, width)
    activ = conv * sig
    slope = sig * (1.0 + conv * (1.0 - sig))
    source = activ * dt_wide
    state = exact_by(nn, b_turned, source * tail)
    first_core = core == 0
    other[...] = jnp.where(first_core, pull, state)
    mine[...] = jnp.where(first_core, state, pull)
    local_copy = remote(
        other, sib_local, (local_sems.at[0], local_sems.at[1]), sibling
    )
    local_copy.start()

    lower = triangle(length, True)
    upper = triangle(length, False)
    lane = lax.broadcasted_iota(jnp.int32, (length, LANES), 1)

    def within():
        turned = cumul.T
        gram = nt(c16, b16)
        gram_turned = nt(b16, c16)
        g_gram = jnp.zeros((length, length), F32)
        g_cumul = jnp.zeros((length, LANES), F32)
        for pair in range(width // LANES):
            at = slice(pair * LANES, (pair + 1) * LANES)
            src_hi, src_lo = split(source[:, at])
            halves = []
            for side in range(2):
                h = 2 * pair + side
                own = lane < HEAD_DIM if side == 0 else lane >= HEAD_DIM
                dy_own = jnp.where(own, dy[:, at], 0.0).astype(BF16)
                col = cumul[:, h : h + 1]
                row = turned[h : h + 1, :]
                decay = jnp.where(lower, jnp.exp(jnp.minimum(col - row, 0.0)), 0.0)
                inside = decay * (nt(dy_own, src_hi) + nt(dy_own, src_lo))
                g_gram = g_gram + inside
                g_cumul = g_cumul + jnp.where(
                    lane == h, jnp.sum(inside * gram, axis=1, keepdims=True), 0.0
                )
                mixing = gram_turned * jnp.where(
                    upper, jnp.exp(jnp.minimum(row - col, 0.0)), 0.0
                )
                halves.append(wide_by(nn, mixing, dy16[:, at]))
            inner[:, at] = jnp.where(lane < HEAD_DIM, halves[0], halves[1])
        gram_sum[...] = g_gram
        cumul_sum[...] = g_cumul

    late = place >= (chips + 1) // 2

    @pl.when(place == 0)
    def _():
        chain_in[...] = jnp.zeros_like(chain_in)

    decay_copy.wait()
    local_copy.wait()

    @pl.when(late)
    def _():
        within()

    def chain_copy(c):
        rows = pl.ds(pl.multiple_of(c * CHUNK, CHUNK), CHUNK)
        return remote(
            chain_out.at[rows, :],
            chain_in.at[rows, :],
            (chain_send.at[c], chain_recv.at[c]),
            ahead,
        )

    def sib_copy(c):
        rows = pl.ds(pl.multiple_of(c * CHUNK, CHUNK), CHUNK)
        return remote(
            sib_out.at[rows, :],
            sib_in.at[rows, :],
            (sib_send.at[c], sib_recv.at[c]),
            sibling,
        )

    def hop(c, _):
        rows = pl.ds(pl.multiple_of(c * CHUNK, CHUNK), CHUNK)

        @pl.when(place > 0)
        def _():
            chain_copy(c).wait_recv()

        here = decay_own[0:1, :] * chain_in[rows, :] + mine[rows, :]
        chain_out[rows, :] = decay_sib[0:1, :] * here + sib_local[rows, :]

        @pl.when(place < chips - 1)
        def _():
            chain_copy(c).start()

        sib_out[rows, :] = here
        sib_copy(c).start()
        return 0

    chunks = STATE // CHUNK
    lax.fori_loop(0, chunks, hop, 0)

    @pl.when(jnp.logical_not(late))
    def _():
        within()

    def drain(c, _):
        @pl.when(place < chips - 1)
        def _():
            chain_copy(c).wait_send()

        sib_copy(c).wait()
        return 0

    lax.fori_loop(0, chunks, drain, 0)

    state = jnp.where(first_core, chain_in[...], sib_in[...])
    pull = jnp.where(first_core, sib_in[...], chain_in[...])
    pulled = tail * exact_by(nn, b16, pull)
    g_source = inner[...] + pulled
    g_conv = (dt_wide * g_source + expand(par_ref[7:8, 0:LANES], width) * dy) * slope
    ext[0:length, :] = g_conv
    top_out[...] = g_conv[0:8, :]
    top_copy = remote(top_out, top_in, (top_sems.at[0], top_sems.at[1]), leading)
    top_copy.start()

    direct = segments(activ * g_source)
    g_cumul = (
        cumul_sum[...] + segments(dy_grown * exact_by(nn, c16, state)) - dt * direct
    )
    carried = jnp.sum(source * pulled, axis=0, keepdims=True) + grow[
        length - 1 : length, :
    ] * jnp.sum(state * pull, axis=0, keepdims=True)
    carried = segments(jnp.broadcast_to(carried, (16, width)))[0:1, :]
    after = jnp.where(upper, 1.0, 0.0).astype(BF16)
    pieces = split(g_cumul, 3)
    later = nn(after, pieces[0]) + (nn(after, pieces[1]) + nn(after, pieces[2]))
    g_dt = direct - rate * (later + carried)
    g_gram = gram_sum[...]
    g_c = wide_by(nn, g_gram, b16) + three(nt, dy_grown, state)
    g_b = wide_by(nn, g_gram.T, c16) + three(nt, source * tail, pull)
    at = width
    for value in (g_b, g_c):
        for part in split(value):
            out_ref[:, at : at + STATE] = part
            at += STATE
    merged = jnp.zeros((length, LANES), F32)
    for j, part in enumerate(split(g_dt, 3)):
        part = part.astype(F32)
        merged = merged + (pltpu.roll(part, j * (width // HEAD_DIM), 1) if j else part)
    out_ref[:, at : at + LANES] = merged.astype(BF16)

    top_copy.wait()
    ext[length : length + 8, :] = jnp.where(me < n_ctx - 1, top_in[...], 0.0)
    g_x = par_ref[3:4, :] * g_conv
    for k in range(CONV - 1):
        g_x = g_x + par_ref[k : k + 1, :] * ext[CONV - 1 - k : CONV - 1 - k + length, :]
    out_ref[:, 0:width] = g_x.astype(BF16)


def shards(x_in, grad_y, b_in, c_in, dt, conv_weight, conv_bias, decay_rate, skip):
    n_head = lax.axis_size("head")
    n_ctx = lax.axis_size("ctx")
    per_group = n_head // GROUPS
    tok_dev = x_in.shape[0]
    heads_dev = decay_rate.shape[0]
    width = heads_dev * HEAD_DIM
    length = tok_dev * n_head

    def spread(value):
        value = value.reshape(tok_dev, GROUPS, 1, STATE)
        value = jnp.broadcast_to(value, (tok_dev, GROUPS, per_group, STATE))
        return value.reshape(tok_dev, n_head, STATE)

    sent = jnp.concatenate(
        [
            x_in.reshape(tok_dev, n_head, width),
            grad_y.reshape(tok_dev, n_head, width),
            spread(b_in),
            spread(c_in),
            jnp.pad(
                dt.reshape(tok_dev, n_head, heads_dev),
                ((0, 0), (0, 0), (0, LANES - heads_dev)),
            ),
        ],
        axis=2,
    )
    total = sent.shape[2]
    rows = lax.all_to_all(
        sent.transpose(1, 0, 2), "head", split_axis=0, concat_axis=0, tiled=True
    ).reshape(length, total)
    wide = lambda value: jnp.pad(value[None, :], ((0, 0), (0, width - heads_dev)))
    params = jnp.concatenate(
        [conv_weight, conv_bias[None, :], conv_bias[None, :], wide(decay_rate), wide(skip)], axis=0
    )
    whole = pltpu.VMEM((STATE, width), F32)
    small = pltpu.VMEM((8, width), F32)
    pair = pltpu.SemaphoreType.DMA((2,))
    many = pltpu.SemaphoreType.DMA((STATE // CHUNK,))
    outs = pl.pallas_call(
        functools.partial(block_kernel, n_ctx),
        out_shape=jax.ShapeDtypeStruct((length, width + 4 * STATE + LANES), BF16),
        in_specs=[pl.BlockSpec(memory_space=pltpu.VMEM)] * 2,
        out_specs=pl.BlockSpec(memory_space=pltpu.VMEM),
        scratch_shapes=[
            pltpu.VMEM((length + 8, width), F32),
            pltpu.VMEM((16, width), BF16),
            small,
            small,
            whole,
            whole,
            whole,
            small,
            small,
            whole,
            whole,
            whole,
            whole,
            pltpu.VMEM((length, length), F32),
            pltpu.VMEM((length, LANES), F32),
            pltpu.VMEM((length, width), F32),
            pair,
            pair,
            pair,
            pair,
            many,
            many,
            many,
            many,
        ],
        compiler_params=pltpu.CompilerParams(
            vmem_limit_bytes=56 * 1024 * 1024, collective_id=0, has_side_effects=True
        ),
    )(rows, params)
    back = lax.all_to_all(
        outs.reshape(n_head, tok_dev, outs.shape[1]),
        "head",
        split_axis=0,
        concat_axis=0,
        tiled=True,
    )
    grad_x = back[:, :, :width].transpose(1, 0, 2).reshape(tok_dev, n_head * width)

    def gathered(at):
        part = back[:, :, at : at + STATE].astype(F32) + back[
            :, :, at + STATE : at + 2 * STATE
        ].astype(F32)
        part = part.reshape(GROUPS, per_group, tok_dev, STATE).sum(axis=1)
        return part.transpose(1, 0, 2).reshape(tok_dev, GROUPS * STATE).astype(BF16)

    at = width + 4 * STATE
    g_dt = back[:, :, at : at + 3 * heads_dev].astype(F32)
    g_dt = g_dt.reshape(n_head, tok_dev, 3, heads_dev).sum(axis=2)
    grad_dt = g_dt.transpose(1, 0, 2).reshape(tok_dev, n_head * heads_dev)
    return (grad_x, gathered(width), gathered(width + 2 * STATE), grad_dt)


def solution(mesh):
    token = P(("ctx", "head"), None)
    in_specs = (token,) * 5 + (P(None, "head"), P("head"), P("head"), P("head"))
    return jax.shard_map(
        shards, mesh=mesh, in_specs=in_specs, out_specs=(token,) * 4, check_vma=False
    )
```

```python
import functools

import jax
import jax.numpy as jnp
from jax import lax
from jax.experimental import pallas as pl
from jax.experimental.pallas import tpu as pltpu
from jax.sharding import PartitionSpec as P

HEAD_DIM = 64
STATE = 256
GROUPS = 8
CONV = 4
LANES = 128
F32 = jnp.float32
BF16 = jnp.bfloat16
MESH = pl.DeviceIdType.MESH
CHUNK = 16


def nn(a, b):
    return lax.dot_general(a, b, (((1,), (0,)), ((), ())), preferred_element_type=F32)


def nt(a, b):
    return lax.dot_general(a, b, (((1,), (1,)), ((), ())), preferred_element_type=F32)


def split(value, pieces=2):
    parts = []
    for _ in range(pieces):
        part = value.astype(BF16)
        parts.append(part)
        value = value - part.astype(F32)
    return parts


def exact_by(dot, exact, wide):
    hi, lo = split(wide)
    return dot(exact, hi) + dot(exact, lo)


def wide_by(dot, wide, exact):
    hi, lo = split(wide)
    return dot(hi, exact) + dot(lo, exact)


def three(dot, left, right):
    lh, ll = split(left)
    rh, rl = split(right)
    return dot(lh, rh) + (dot(lh, rl) + dot(ll, rh))


def expand(cols, width):
    lane = lax.broadcasted_iota(jnp.int32, (cols.shape[0], LANES), 1)
    parts = [
        jnp.where(lane < HEAD_DIM, cols[:, h : h + 1], cols[:, h + 1 : h + 2])
        for h in range(0, width // HEAD_DIM, 2)
    ]
    return jnp.concatenate(parts, axis=1)


def segments(value):
    width = value.shape[1]
    row = lax.broadcasted_iota(jnp.int32, (width, LANES), 0)
    col = lax.broadcasted_iota(jnp.int32, (width, LANES), 1)
    pick = jnp.where(
        (row >= col * HEAD_DIM) & (row < (col + 1) * HEAD_DIM), 1.0, 0.0
    ).astype(BF16)
    return wide_by(nn, value, pick)


def triangle(length, lower):
    row = lax.broadcasted_iota(jnp.int32, (length, length), 0)
    col = lax.broadcasted_iota(jnp.int32, (length, length), 1)
    return row >= col if lower else row <= col


def convolve(x, par_ref, ext):
    length = x.shape[0]
    ext[8 : 8 + length, :] = x
    conv = par_ref[4:5, :] + par_ref[0:1, :] * ext[5 : 5 + length, :]
    for k in range(1, CONV):
        conv = conv + par_ref[k : k + 1, :] * ext[5 + k : 5 + k + length, :]
    return conv, 1.0 / (1.0 + jnp.exp(-conv))


def flat(ref):
    value = ref[...].astype(F32)
    return value.reshape(value.shape[0] * value.shape[1], value.shape[2])


def block_kernel(
    n_ctx,
    n_head,
    x_ref,
    dy_ref,
    b_ref,
    c_ref,
    dt_ref,
    par_ref,
    gx_ref,
    gb_ref,
    gc_ref,
    gdt_ref,
    x_buf,
    dy_buf,
    b_buf,
    c_buf,
    dt_buf,
    gx_buf,
    gb_buf,
    gc_buf,
    gdt_buf,
    gb_all,
    gc_all,
    gdt_all,
    head_send,
    head_recv,
    ext,
    edge,
    top_out,
    top_in,
    mine,
    other,
    sib_local,
    decay_own,
    decay_sib,
    chain_in,
    chain_out,
    sib_out,
    sib_in,
    gram_sum,
    cumul_sum,
    inner,
    edge_sems,
    top_sems,
    local_sems,
    decay_sems,
    chain_send,
    chain_recv,
    sib_send,
    sib_recv,
):
    length, width = ext.shape[0] - 8, ext.shape[1]
    tok_dev = x_ref.shape[0]
    heads_dev = width // HEAD_DIM
    per_group = n_head // GROUPS
    per_tile = LANES // heads_dev
    head = lax.axis_index("head")
    me = lax.axis_index("ctx")
    core = lax.rem(me, 2)
    chip = lax.div(me, 2)
    chips = n_ctx // 2
    sign = 1 - 2 * core
    place = core * (chips - 1) + sign * chip
    sibling = me + sign
    ahead = lax.rem(me + 2 * sign + n_ctx, n_ctx)
    following = lax.rem(me + 1, n_ctx)
    leading = lax.rem(me + n_ctx - 1, n_ctx)

    def remote(src, dst, sems, device, axis="ctx"):
        return pltpu.make_async_remote_copy(
            src_ref=src,
            dst_ref=dst,
            send_sem=sems[0],
            recv_sem=sems[1],
            device_id={axis: device},
            device_id_type=MESH,
        )

    barrier = pltpu.get_barrier_semaphore()
    for by in (1, 2, n_ctx - 2, n_ctx - 1):
        pl.semaphore_signal(
            barrier,
            inc=1,
            device_id={"ctx": lax.rem(me + by, n_ctx)},
            device_id_type=MESH,
        )

    def greet(k, _):
        pl.semaphore_signal(
            barrier,
            inc=1,
            device_id={"head": lax.rem(head + k, n_head)},
            device_id_type=MESH,
        )
        return 0

    lax.fori_loop(1, n_head, greet, 0)
    pl.semaphore_wait(barrier, 3 + n_head)

    def scatter(kind, source, target):
        def step(k, _):
            to = lax.rem(head + k, n_head)
            remote(
                source(to), target, (head_send.at[kind], head_recv.at[kind]), to, "head"
            ).start()
            return 0

        lax.fori_loop(1, n_head, step, 0)
        pltpu.make_async_copy(source(head), target, head_recv.at[kind]).start()

    def arrived(kind, buffer):
        pltpu.make_async_copy(buffer, buffer, head_recv.at[kind]).wait()

    def sent(kind, buffer):
        part = buffer.at[0 : n_head - 1]
        pltpu.make_async_copy(part, part, head_send.at[kind]).wait()

    def lanes(ref, start, size):
        return ref.at[:, pl.ds(pl.multiple_of(start, LANES), size)]

    scatter(0, lambda to: lanes(b_ref, lax.div(to, per_group) * STATE, STATE), b_buf.at[head])
    scatter(1, lambda to: lanes(c_ref, lax.div(to, per_group) * STATE, STATE), c_buf.at[head])
    scatter(2, lambda to: lanes(dt_ref, lax.div(to, per_tile) * LANES, LANES), dt_buf.at[head])
    scatter(3, lambda to: lanes(x_ref, to * width, width), x_buf.at[head])
    scatter(4, lambda to: lanes(dy_ref, to * width, width), dy_buf.at[head])

    lower = triangle(length, True)
    upper = triangle(length, False)
    lane = lax.broadcasted_iota(jnp.int32, (length, LANES), 1)
    arrived(0, b_buf)
    arrived(1, c_buf)
    arrived(2, dt_buf)
    shift = lax.rem(LANES - lax.rem(head, per_tile) * heads_dev, LANES)
    dt = jnp.where(lane < heads_dev, pltpu.roll(flat(dt_buf), shift, 1), 0.0)
    rate = par_ref[6:7, 0:LANES]
    cumul = -rate * nn(jnp.where(lower, 1.0, 0.0).astype(BF16), dt.astype(BF16))
    grow = expand(jnp.exp(cumul), width)
    tail = expand(jnp.exp(cumul[length - 1 : length, :] - cumul), width)
    dt_wide = expand(dt, width)
    b32 = flat(b_buf)
    c32 = flat(c_buf)
    b16 = b32.astype(BF16)
    c16 = c32.astype(BF16)
    b_turned = b32.T.astype(BF16)
    c_turned = c32.T.astype(BF16)
    decay_own[...] = jnp.broadcast_to(grow[length - 1 : length, :], (8, width))
    decay_copy = remote(
        decay_own, decay_sib, (decay_sems.at[0], decay_sems.at[1]), sibling
    )
    decay_copy.start()
    arrived(3, x_buf)
    edge_copy = remote(
        x_buf.at[n_head - 1, tok_dev - 8 : tok_dev, :],
        edge,
        (edge_sems.at[0], edge_sems.at[1]),
        following,
    )
    edge_copy.start()
    arrived(4, dy_buf)
    dy = flat(dy_buf)
    dy16 = dy.astype(BF16)
    dy_grown = dy * grow
    pull = exact_by(nn, c_turned, dy_grown)

    edge_copy.wait()
    ext[0:8, :] = jnp.where(me > 0, edge[...].astype(F32), 0.0)
    conv, sig = convolve(flat(x_buf), par_ref, ext)
    activ = conv * sig
    slope = sig * (1.0 + conv * (1.0 - sig))
    source = activ * dt_wide
    state = exact_by(nn, b_turned, source * tail)
    first_core = core == 0
    other[...] = jnp.where(first_core, pull, state)
    mine[...] = jnp.where(first_core, state, pull)
    local_copy = remote(
        other, sib_local, (local_sems.at[0], local_sems.at[1]), sibling
    )
    local_copy.start()

    def within():
        turned = cumul.T
        gram = nt(c16, b16)
        gram_turned = nt(b16, c16)
        g_gram = jnp.zeros((length, length), F32)
        g_cumul = jnp.zeros((length, LANES), F32)
        for pair in range(width // LANES):
            at = slice(pair * LANES, (pair + 1) * LANES)
            src_hi, src_lo = split(source[:, at])
            halves = []
            for side in range(2):
                h = 2 * pair + side
                own = lane < HEAD_DIM if side == 0 else lane >= HEAD_DIM
                dy_own = jnp.where(own, dy[:, at], 0.0).astype(BF16)
                col = cumul[:, h : h + 1]
                row = turned[h : h + 1, :]
                decay = jnp.where(lower, jnp.exp(jnp.minimum(col - row, 0.0)), 0.0)
                inside = decay * (nt(dy_own, src_hi) + nt(dy_own, src_lo))
                g_gram = g_gram + inside
                g_cumul = g_cumul + jnp.where(
                    lane == h, jnp.sum(inside * gram, axis=1, keepdims=True), 0.0
                )
                mixing = gram_turned * jnp.where(
                    upper, jnp.exp(jnp.minimum(row - col, 0.0)), 0.0
                )
                halves.append(wide_by(nn, mixing, dy16[:, at]))
            inner[:, at] = jnp.where(lane < HEAD_DIM, halves[0], halves[1])
        gram_sum[...] = g_gram
        cumul_sum[...] = g_cumul

    late = place >= (chips + 1) // 2

    @pl.when(place == 0)
    def _():
        chain_in[...] = jnp.zeros_like(chain_in)

    decay_copy.wait()
    local_copy.wait()

    @pl.when(late)
    def _():
        within()

    def chain_copy(c):
        rows = pl.ds(pl.multiple_of(c * CHUNK, CHUNK), CHUNK)
        return remote(
            chain_out.at[rows, :],
            chain_in.at[rows, :],
            (chain_send.at[c], chain_recv.at[c]),
            ahead,
        )

    def sib_copy(c):
        rows = pl.ds(pl.multiple_of(c * CHUNK, CHUNK), CHUNK)
        return remote(
            sib_out.at[rows, :],
            sib_in.at[rows, :],
            (sib_send.at[c], sib_recv.at[c]),
            sibling,
        )

    def hop(c, _):
        rows = pl.ds(pl.multiple_of(c * CHUNK, CHUNK), CHUNK)

        @pl.when(place > 0)
        def _():
            chain_copy(c).wait_recv()

        here = decay_own[0:1, :] * chain_in[rows, :] + mine[rows, :]
        chain_out[rows, :] = decay_sib[0:1, :] * here + sib_local[rows, :]

        @pl.when(place < chips - 1)
        def _():
            chain_copy(c).start()

        sib_out[rows, :] = here
        sib_copy(c).start()
        return 0

    chunks = STATE // CHUNK
    lax.fori_loop(0, chunks, hop, 0)

    @pl.when(jnp.logical_not(late))
    def _():
        within()

    def drain(c, _):
        @pl.when(place < chips - 1)
        def _():
            chain_copy(c).wait_send()

        sib_copy(c).wait()
        return 0

    lax.fori_loop(0, chunks, drain, 0)

    state = jnp.where(first_core, chain_in[...], sib_in[...])
    pull = jnp.where(first_core, sib_in[...], chain_in[...])
    pulled = tail * exact_by(nn, b16, pull)
    g_source = inner[...] + pulled
    g_conv = (dt_wide * g_source + expand(par_ref[7:8, 0:LANES], width) * dy) * slope
    ext[0:length, :] = g_conv
    top_out[...] = g_conv[0:8, :]
    top_copy = remote(top_out, top_in, (top_sems.at[0], top_sems.at[1]), leading)
    top_copy.start()

    def by_token(value):
        return value.reshape(n_head, tok_dev, value.shape[1])

    g_gram = gram_sum[...]
    gb_buf[...] = by_token(
        wide_by(nn, g_gram.T, c16) + three(nt, source * tail, pull)
    )
    scatter(5, lambda to: gb_buf.at[to], gb_all.at[head])
    gc_buf[...] = by_token(wide_by(nn, g_gram, b16) + three(nt, dy_grown, state))
    scatter(6, lambda to: gc_buf.at[to], gc_all.at[head])

    top_copy.wait()
    ext[length : length + 8, :] = jnp.where(me < n_ctx - 1, top_in[...], 0.0)
    g_x = par_ref[3:4, :] * g_conv
    for k in range(CONV - 1):
        g_x = g_x + par_ref[k : k + 1, :] * ext[CONV - 1 - k : CONV - 1 - k + length, :]
    gx_buf[...] = by_token(g_x).astype(BF16)
    scatter(7, lambda to: gx_buf.at[to], lanes(gx_ref, head * width, width))

    direct = segments(activ * g_source)
    g_cumul = (
        cumul_sum[...] + segments(dy_grown * exact_by(nn, c16, state)) - dt * direct
    )
    carried = jnp.sum(source * pulled, axis=0, keepdims=True) + grow[
        length - 1 : length, :
    ] * jnp.sum(state * pull, axis=0, keepdims=True)
    carried = segments(jnp.broadcast_to(carried, (16, width)))[0:1, :]
    after = jnp.where(upper, 1.0, 0.0).astype(BF16)
    pieces = split(g_cumul, 3)
    later = nn(after, pieces[0]) + (nn(after, pieces[1]) + nn(after, pieces[2]))
    g_dt = direct - rate * (later + carried)
    merged = jnp.zeros((length, LANES), F32)
    for j, part in enumerate(split(g_dt, 3)):
        part = part.astype(F32)
        merged = merged + (pltpu.roll(part, j * heads_dev, 1) if j else part)
    gdt_buf[...] = by_token(merged).astype(BF16)
    scatter(8, lambda to: gdt_buf.at[to], gdt_all.at[head])

    for kind, buffer, result in ((5, gb_all, gb_ref), (6, gc_all, gc_ref)):
        arrived(kind, buffer)
        for g in range(GROUPS):
            summed = buffer[g * per_group]
            for j in range(1, per_group):
                summed = summed + buffer[g * per_group + j]
            result[:, g * STATE : (g + 1) * STATE] = summed.astype(BF16)
    arrived(8, gdt_all)
    own = lax.broadcasted_iota(jnp.int32, (tok_dev, LANES), 1) < heads_dev
    for tile in range(n_head // per_tile):
        summed = jnp.zeros((tok_dev, LANES), F32)
        for j in range(per_tile):
            value = gdt_all[tile * per_tile + j].astype(F32)
            value = (
                value
                + pltpu.roll(value, LANES - heads_dev, 1)
                + pltpu.roll(value, LANES - 2 * heads_dev, 1)
            )
            value = jnp.where(own, value, 0.0)
            summed = summed + (pltpu.roll(value, j * heads_dev, 1) if j else value)
        gdt_ref[:, tile * LANES : (tile + 1) * LANES] = summed
    arrived(7, gx_ref)
    for kind, buffer in enumerate(
        (b_buf, c_buf, dt_buf, x_buf, dy_buf, gb_buf, gc_buf, gx_buf, gdt_buf)
    ):
        sent(kind, buffer)


def shards(x_in, grad_y, b_in, c_in, dt, conv_weight, conv_bias, decay_rate, skip):
    n_head = lax.axis_size("head")
    n_ctx = lax.axis_size("ctx")
    per_group = n_head // GROUPS
    tok_dev = x_in.shape[0]
    heads_dev = decay_rate.shape[0]
    width = heads_dev * HEAD_DIM
    length = tok_dev * n_head

    wide = lambda value: jnp.pad(value[None, :], ((0, 0), (0, width - heads_dev)))
    params = jnp.concatenate(
        [conv_weight, conv_bias[None, :], conv_bias[None, :], wide(decay_rate), wide(skip)], axis=0
    )
    whole = pltpu.VMEM((STATE, width), F32)
    small = pltpu.VMEM((8, width), F32)
    held = lambda size, kind: pltpu.VMEM((n_head, tok_dev, size), kind)
    pair = pltpu.SemaphoreType.DMA((2,))
    many = pltpu.SemaphoreType.DMA((STATE // CHUNK,))
    return pl.pallas_call(
        functools.partial(block_kernel, n_ctx, n_head),
        out_shape=(
            jax.ShapeDtypeStruct(x_in.shape, BF16),
            jax.ShapeDtypeStruct(b_in.shape, BF16),
            jax.ShapeDtypeStruct(c_in.shape, BF16),
            jax.ShapeDtypeStruct(dt.shape, F32),
        ),
        in_specs=[pl.BlockSpec(memory_space=pltpu.VMEM)] * 6,
        out_specs=[pl.BlockSpec(memory_space=pltpu.VMEM)] * 4,
        scratch_shapes=[
            held(width, BF16),
            held(width, BF16),
            held(STATE, BF16),
            held(STATE, BF16),
            held(LANES, BF16),
            held(width, BF16),
            held(STATE, F32),
            held(STATE, F32),
            held(LANES, BF16),
            held(STATE, F32),
            held(STATE, F32),
            held(LANES, BF16),
            pltpu.SemaphoreType.DMA((9,)),
            pltpu.SemaphoreType.DMA((9,)),
            pltpu.VMEM((length + 8, width), F32),
            pltpu.VMEM((8, width), BF16),
            small,
            small,
            whole,
            whole,
            whole,
            small,
            small,
            whole,
            whole,
            whole,
            whole,
            pltpu.VMEM((length, length), F32),
            pltpu.VMEM((length, LANES), F32),
            pltpu.VMEM((length, width), F32),
            pair,
            pair,
            pair,
            pair,
            many,
            many,
            many,
            many,
        ],
        compiler_params=pltpu.CompilerParams(
            vmem_limit_bytes=56 * 1024 * 1024, collective_id=0, has_side_effects=True
        ),
    )(x_in, grad_y, b_in, c_in, dt, params)


def solution(mesh):
    token = P(("ctx", "head"), None)
    in_specs = (token,) * 5 + (P(None, "head"), P("head"), P("head"), P("head"))
    return jax.shard_map(
        shards, mesh=mesh, in_specs=in_specs, out_specs=(token,) * 4, check_vma=False
    )
```

```python
import functools

import jax
import jax.numpy as jnp
from jax import lax
from jax.experimental import pallas as pl
from jax.experimental.pallas import tpu as pltpu
from jax.sharding import PartitionSpec as P

HEAD_DIM = 64
STATE = 256
GROUPS = 8
CONV = 4
LANES = 128
F32 = jnp.float32
BF16 = jnp.bfloat16
MESH = pl.DeviceIdType.MESH
PIECES = 4
CHUNK = 16 * PIECES


def nn(a, b):
    return lax.dot_general(a, b, (((1,), (0,)), ((), ())), preferred_element_type=F32)


def nt(a, b):
    return lax.dot_general(a, b, (((1,), (1,)), ((), ())), preferred_element_type=F32)


def split(value, pieces=2):
    parts = []
    for _ in range(pieces):
        part = value.astype(BF16)
        parts.append(part)
        value = value - part.astype(F32)
    return parts


def exact_by(dot, exact, wide):
    hi, lo = split(wide)
    return dot(exact, hi) + dot(exact, lo)


def wide_by(dot, wide, exact):
    hi, lo = split(wide)
    return dot(hi, exact) + dot(lo, exact)


def three(dot, left, right):
    lh, ll = split(left)
    rh, rl = split(right)
    return dot(lh, rh) + (dot(lh, rl) + dot(ll, rh))


def expand(cols, width, first=0):
    lane = lax.broadcasted_iota(jnp.int32, (cols.shape[0], LANES), 1)
    parts = [
        jnp.where(lane < HEAD_DIM, cols[:, h : h + 1], cols[:, h + 1 : h + 2])
        for h in range(first, first + width // HEAD_DIM, 2)
    ]
    return jnp.concatenate(parts, axis=1)


def segments(value, first=0):
    width = value.shape[1]
    row = lax.broadcasted_iota(jnp.int32, (width, LANES), 0)
    col = lax.broadcasted_iota(jnp.int32, (width, LANES), 1) - first
    pick = jnp.where(
        (row >= col * HEAD_DIM) & (row < (col + 1) * HEAD_DIM), 1.0, 0.0
    ).astype(BF16)
    return wide_by(nn, value, pick)


def triangle(length, lower):
    row = lax.broadcasted_iota(jnp.int32, (length, length), 0)
    col = lax.broadcasted_iota(jnp.int32, (length, length), 1)
    return row >= col if lower else row <= col


def convolve(x, par_ref, cols, ext):
    length = x.shape[0]
    ext[8 : 8 + length, :] = x
    conv = par_ref[4:5, cols] + par_ref[0:1, cols] * ext[5 : 5 + length, :]
    for k in range(1, CONV):
        conv = conv + par_ref[k : k + 1, cols] * ext[5 + k : 5 + k + length, :]
    return conv, 1.0 / (1.0 + jnp.exp(-conv))


def flat(ref):
    value = ref[...].astype(F32)
    return value.reshape(value.shape[0] * value.shape[1], value.shape[2])


def block_kernel(
    n_ctx,
    n_head,
    x_ref,
    dy_ref,
    b_ref,
    c_ref,
    dt_ref,
    par_ref,
    gx_ref,
    gb_ref,
    gc_ref,
    gdt_ref,
    x_buf,
    dy_buf,
    b_buf,
    c_buf,
    dt_buf,
    gx_buf,
    gb_buf,
    gc_buf,
    gdt_buf,
    gb_all,
    gc_all,
    gdt_all,
    head_send,
    head_recv,
    ext,
    edge,
    top_out,
    top_in,
    mine,
    other,
    sib_local,
    decay_own,
    decay_sib,
    chain_in,
    chain_out,
    sib_out,
    sib_in,
    gram_sum,
    cumul_sum,
    inner,
    edge_sems,
    top_sems,
    local_sems,
    decay_sems,
    chain_send,
    chain_recv,
    sib_send,
    sib_recv,
):
    pieces, length, part = ext.shape[0], ext.shape[1] - 8, ext.shape[2]
    width = pieces * part
    tok_dev = x_ref.shape[0]
    heads_dev = width // HEAD_DIM
    per_group = n_head // GROUPS
    per_tile = LANES // heads_dev
    head = lax.axis_index("head")
    me = lax.axis_index("ctx")
    core = lax.rem(me, 2)
    chip = lax.div(me, 2)
    chips = n_ctx // 2
    sign = 1 - 2 * core
    place = core * (chips - 1) + sign * chip
    sibling = me + sign
    per_piece = part // HEAD_DIM
    chunks = STATE // CHUNK
    pace = max(chips // pieces, 1)
    lag = lax.div(place + pace - 1, pace)
    late = place >= max(chips // 2 - 1, 1)
    early = jnp.logical_not(late)
    ahead = lax.rem(me + 2 * sign + n_ctx, n_ctx)
    following = lax.rem(me + 1, n_ctx)
    leading = lax.rem(me + n_ctx - 1, n_ctx)

    def remote(src, dst, sems, device, axis="ctx"):
        return pltpu.make_async_remote_copy(
            src_ref=src,
            dst_ref=dst,
            send_sem=sems[0],
            recv_sem=sems[1],
            device_id={axis: device},
            device_id_type=MESH,
        )

    barrier = pltpu.get_barrier_semaphore()
    for by in (1, 2, n_ctx - 2, n_ctx - 1):
        pl.semaphore_signal(
            barrier,
            inc=1,
            device_id={"ctx": lax.rem(me + by, n_ctx)},
            device_id_type=MESH,
        )

    def greet(k, _):
        pl.semaphore_signal(
            barrier,
            inc=1,
            device_id={"head": lax.rem(head + k, n_head)},
            device_id_type=MESH,
        )
        return 0

    lax.fori_loop(1, n_head, greet, 0)
    pl.semaphore_wait(barrier, 3 + n_head)

    def scatter(kind, source, target):
        def step(k, _):
            to = lax.rem(head + k, n_head)
            remote(
                source(to), target, (head_send.at[kind], head_recv.at[kind]), to, "head"
            ).start()
            return 0

        lax.fori_loop(1, n_head, step, 0)
        pltpu.make_async_copy(source(head), target, head_recv.at[kind]).start()

    def arrived(kind, buffer):
        pltpu.make_async_copy(buffer, buffer, head_recv.at[kind]).wait()

    def sent(kind, buffer):
        pltpu.make_async_copy(buffer, buffer, head_send.at[kind]).wait()

    def lanes(ref, start, size):
        return ref.at[:, pl.ds(pl.multiple_of(start, LANES), size)]

    def send_piece(kind, ref, buffer, p):
        scatter(
            kind + p,
            lambda to: lanes(ref, to * width + p * part, part),
            buffer.at[p, head],
        )

    x_kind, dy_kind, out_kind = 3, 3 + pieces, 3 + 2 * pieces
    scatter(2, lambda to: lanes(dt_ref, lax.div(to, per_tile) * LANES, LANES), dt_buf.at[head])
    scatter(0, lambda to: lanes(b_ref, lax.div(to, per_group) * STATE, STATE), b_buf.at[head])
    scatter(1, lambda to: lanes(c_ref, lax.div(to, per_group) * STATE, STATE), c_buf.at[head])
    send_piece(x_kind, x_ref, x_buf, 0)
    for p in range(pieces):
        if p + 1 < pieces:
            send_piece(x_kind, x_ref, x_buf, p + 1)
        send_piece(dy_kind, dy_ref, dy_buf, p)

    @pl.when(place == 0)
    def _():
        chain_in[...] = jnp.zeros_like(chain_in)

    def edge_copy(p):
        return remote(
            x_buf.at[p, n_head - 1, tok_dev - 8 : tok_dev, :],
            edge.at[p],
            (edge_sems.at[0, p], edge_sems.at[1, p]),
            following,
        )

    def local_copy(p):
        return remote(
            other.at[p], sib_local.at[p], (local_sems.at[0, p], local_sems.at[1, p]), sibling
        )

    def top_copy(p):
        return remote(
            top_out.at[p], top_in.at[p], (top_sems.at[0, p], top_sems.at[1, p]), leading
        )

    def chain_copy(p, c):
        rows = pl.ds(pl.multiple_of(c * CHUNK, CHUNK), CHUNK)
        return remote(
            chain_out.at[p, rows, :],
            chain_in.at[p, rows, :],
            (chain_send.at[p, c], chain_recv.at[p, c]),
            ahead,
        )

    def sib_copy(p, c):
        rows = pl.ds(pl.multiple_of(c * CHUNK, CHUNK), CHUNK)
        return remote(
            sib_out.at[p, rows, :],
            sib_in.at[p, rows, :],
            (sib_send.at[p, c], sib_recv.at[p, c]),
            sibling,
        )

    lower = triangle(length, True)
    upper = triangle(length, False)
    lane = lax.broadcasted_iota(jnp.int32, (length, LANES), 1)
    arrived(2, dt_buf)
    shift = lax.rem(LANES - lax.rem(head, per_tile) * heads_dev, LANES)
    dt = jnp.where(lane < heads_dev, pltpu.roll(flat(dt_buf), shift, 1), 0.0)
    rate = par_ref[6:7, 0:LANES]
    cumul = -rate * nn(jnp.where(lower, 1.0, 0.0).astype(BF16), dt.astype(BF16))
    grow_cols = jnp.exp(cumul)
    tail_cols = jnp.exp(cumul[length - 1 : length, :] - cumul)
    for p in range(pieces):
        last = expand(grow_cols[length - 8 : length, :], part, p * per_piece)
        decay_own[p] = jnp.broadcast_to(last[7:8, :], (8, part))
    decay_copy = remote(
        decay_own, decay_sib, (decay_sems.at[0], decay_sems.at[1]), sibling
    )
    decay_copy.start()
    arrived(0, b_buf)
    arrived(1, c_buf)
    b32 = flat(b_buf)
    c32 = flat(c_buf)
    b16 = b32.astype(BF16)
    c16 = c32.astype(BF16)
    b_turned = b32.T.astype(BF16)
    c_turned = c32.T.astype(BF16)
    turned = cumul.T
    gram = nt(c16, b16)
    gram_turned = nt(b16, c16)
    gram_sum[...] = jnp.zeros_like(gram_sum)
    cumul_sum[...] = jnp.zeros_like(cumul_sum)
    first_core = core == 0

    def local(p):
        if p == 0:
            arrived(x_kind, x_buf.at[0])
            edge_copy(0).start()
        if p + 1 < pieces:
            arrived(x_kind + p + 1, x_buf.at[p + 1])
            edge_copy(p + 1).start()
        arrived(dy_kind + p, dy_buf.at[p])
        cols = slice(p * part, (p + 1) * part)
        dy = flat(dy_buf.at[p])
        grow = expand(grow_cols, part, p * per_piece)
        tail = expand(tail_cols, part, p * per_piece)
        dt_wide = expand(dt, part, p * per_piece)
        dy_grown = dy * grow
        pull = exact_by(nn, c_turned, dy_grown)
        edge_copy(p).wait()
        ext[p, 0:8, :] = jnp.where(me > 0, edge[p].astype(F32), 0.0)
        conv, sig = convolve(flat(x_buf.at[p]), par_ref, cols, ext.at[p])
        activ = conv * sig
        slope = sig * (1.0 + conv * (1.0 - sig))
        source = activ * dt_wide
        state = exact_by(nn, b_turned, source * tail)
        other[p] = jnp.where(first_core, pull, state)
        local_copy(p).start()
        mine[p] = jnp.where(first_core, state, pull)
        return (cols, dy, grow, tail, dt_wide, dy_grown, activ, slope, source)

    def chain(p):
        local_copy(p).wait_recv()

        def hop(c, _):
            rows = pl.ds(pl.multiple_of(c * CHUNK, CHUNK), CHUNK)

            @pl.when(place > 0)
            def _():
                chain_copy(p, c).wait_recv()

            here = decay_own[p, 0:1, :] * chain_in[p, rows, :] + mine[p, rows, :]
            chain_out[p, rows, :] = decay_sib[p, 0:1, :] * here + sib_local[p, rows, :]

            @pl.when(place < chips - 1)
            def _():
                chain_copy(p, c).start()

            sib_out[p, rows, :] = here
            sib_copy(p, c).start()
            return 0

        lax.fori_loop(0, chunks, hop, 0)

    def within(p):
        dy, source = held[p][1], held[p][8]
        g_gram = gram_sum[...]
        g_cumul = cumul_sum[...]
        for pair in range(part // LANES):
            at = slice(pair * LANES, (pair + 1) * LANES)
            src_hi, src_lo = split(source[:, at])
            dy16 = dy[:, at].astype(BF16)
            halves = []
            for side in range(2):
                h = p * per_piece + 2 * pair + side
                own = lane < HEAD_DIM if side == 0 else lane >= HEAD_DIM
                dy_own = jnp.where(own, dy[:, at], 0.0).astype(BF16)
                col = cumul[:, h : h + 1]
                row = turned[h : h + 1, :]
                decay = jnp.where(lower, jnp.exp(jnp.minimum(col - row, 0.0)), 0.0)
                inside = decay * (nt(dy_own, src_hi) + nt(dy_own, src_lo))
                g_gram = g_gram + inside
                g_cumul = g_cumul + jnp.where(
                    lane == h, jnp.sum(inside * gram, axis=1, keepdims=True), 0.0
                )
                mixing = gram_turned * jnp.where(
                    upper, jnp.exp(jnp.minimum(row - col, 0.0)), 0.0
                )
                halves.append(wide_by(nn, mixing, dy16))
            inner[p, :, at] = jnp.where(lane < HEAD_DIM, halves[0], halves[1])
        gram_sum[...] = g_gram
        cumul_sum[...] = g_cumul

    held = []
    for step in range(pieces):
        held.append(local(step))
        if step == 0:
            decay_copy.wait()

        @pl.when(step >= lag)
        def _():
            chain(step - lag)

        if step + 1 < pieces:
            within(step)

    @pl.when(late)
    def _():
        within(pieces - 1)

    for j in range(1, pieces):

        @pl.when(early & (lag >= j))
        def _():
            chain(pieces - 1 - lag + j)

    @pl.when(early)
    def _():
        within(pieces - 1)

    def by_token(value):
        return value.reshape(n_head, tok_dev, value.shape[1])

    def finish(p):
        cols = held[p][0]
        top_copy(p).wait()
        ext[p, length : length + 8, :] = jnp.where(me < n_ctx - 1, top_in[p], 0.0)
        g_x = par_ref[3:4, cols] * ext[p, 0:length, :]
        for k in range(CONV - 1):
            back = CONV - 1 - k
            g_x = g_x + par_ref[k : k + 1, cols] * ext[p, back : back + length, :]
        gx_buf[p] = by_token(g_x).astype(BF16)
        scatter(
            out_kind + 3,
            lambda to: gx_buf.at[p, to],
            lanes(gx_ref, head * width + p * part, part),
        )

    g_gram = gram_sum[...]
    g_b = wide_by(nn, g_gram.T, c16)
    g_c = wide_by(nn, g_gram, b16)
    direct = jnp.zeros((length, LANES), F32)
    g_cumul = cumul_sum[...]
    total = jnp.zeros((16, LANES), F32)
    for p in range(pieces):

        @pl.when(late & (lag > pieces - 1 - p))
        def _():
            chain(p)

        lax.fori_loop(0, chunks, lambda c, _: (sib_copy(p, c).wait_recv(), 0)[1], 0)
        cols, dy, grow, tail, dt_wide, dy_grown, activ, slope, source = held[p]
        state = jnp.where(first_core, chain_in[p], sib_in[p])
        pull = jnp.where(first_core, sib_in[p], chain_in[p])
        pulled = tail * exact_by(nn, b16, pull)
        g_source = inner[p] + pulled
        skip = expand(par_ref[7:8, 0:LANES], part, p * per_piece)
        g_conv = (dt_wide * g_source + skip * dy) * slope
        ext[p, 0:length, :] = g_conv
        top_out[p] = g_conv[0:8, :]
        top_copy(p).start()
        g_b = g_b + three(nt, source * tail, pull)
        g_c = g_c + three(nt, dy_grown, state)
        if p + 1 == pieces:
            gb_buf[...] = by_token(g_b)
            scatter(out_kind, lambda to: gb_buf.at[to], gb_all.at[head])
            gc_buf[...] = by_token(g_c)
            scatter(out_kind + 1, lambda to: gc_buf.at[to], gc_all.at[head])
        first = p * per_piece
        direct = direct + segments(activ * g_source, first)
        g_cumul = g_cumul + segments(dy_grown * exact_by(nn, c16, state), first)
        carried = jnp.sum(source * pulled, axis=0, keepdims=True) + grow[
            length - 1 : length, :
        ] * jnp.sum(state * pull, axis=0, keepdims=True)
        total = total + segments(jnp.broadcast_to(carried, (16, part)), first)
        if p > 0:
            finish(p - 1)
    finish(pieces - 1)

    after = jnp.where(upper, 1.0, 0.0).astype(BF16)
    terms = split(g_cumul - dt * direct, 3)
    later = nn(after, terms[0]) + (nn(after, terms[1]) + nn(after, terms[2]))
    g_dt = direct - rate * (later + total[0:1, :])
    merged = jnp.zeros((length, LANES), F32)
    for j, term in enumerate(split(g_dt, 3)):
        term = term.astype(F32)
        merged = merged + (pltpu.roll(term, j * heads_dev, 1) if j else term)
    gdt_buf[...] = by_token(merged).astype(BF16)
    scatter(out_kind + 2, lambda to: gdt_buf.at[to], gdt_all.at[head])

    for kind, buffer, result in ((out_kind, gb_all, gb_ref), (out_kind + 1, gc_all, gc_ref)):
        arrived(kind, buffer)
        for g in range(GROUPS):
            summed = buffer[g * per_group]
            for j in range(1, per_group):
                summed = summed + buffer[g * per_group + j]
            result[:, g * STATE : (g + 1) * STATE] = summed.astype(BF16)
    arrived(out_kind + 2, gdt_all)
    own = lax.broadcasted_iota(jnp.int32, (tok_dev, LANES), 1) < heads_dev
    for tile in range(n_head // per_tile):
        summed = jnp.zeros((tok_dev, LANES), F32)
        for j in range(per_tile):
            value = gdt_all[tile * per_tile + j].astype(F32)
            value = (
                value
                + pltpu.roll(value, LANES - heads_dev, 1)
                + pltpu.roll(value, LANES - 2 * heads_dev, 1)
            )
            value = jnp.where(own, value, 0.0)
            summed = summed + (pltpu.roll(value, j * heads_dev, 1) if j else value)
        gdt_ref[:, tile * LANES : (tile + 1) * LANES] = summed
    arrived(out_kind + 3, gx_ref)

    for kind, buffer in enumerate((b_buf, c_buf, dt_buf)):
        sent(kind, buffer.at[0 : n_head - 1])
    for p in range(pieces):
        sent(x_kind + p, x_buf.at[p, 0 : n_head - 1])
        sent(dy_kind + p, dy_buf.at[p, 0 : n_head - 1])
        local_copy(p).wait_send()

        def drain(c, _):
            @pl.when(place < chips - 1)
            def _():
                chain_copy(p, c).wait_send()

            sib_copy(p, c).wait_send()
            return 0

        lax.fori_loop(0, chunks, drain, 0)
    for kind, buffer in enumerate((gb_buf, gc_buf, gdt_buf)):
        sent(out_kind + kind, buffer.at[0 : n_head - 1])
    sent(out_kind + 3, gx_buf.at[:, 0 : n_head - 1])


def shards(x_in, grad_y, b_in, c_in, dt, conv_weight, conv_bias, decay_rate, skip):
    n_head = lax.axis_size("head")
    n_ctx = lax.axis_size("ctx")
    per_group = n_head // GROUPS
    tok_dev = x_in.shape[0]
    heads_dev = decay_rate.shape[0]
    width = heads_dev * HEAD_DIM
    length = tok_dev * n_head

    wide = lambda value: jnp.pad(value[None, :], ((0, 0), (0, width - heads_dev)))
    params = jnp.concatenate(
        [conv_weight, conv_bias[None, :], conv_bias[None, :], wide(decay_rate), wide(skip)], axis=0
    )
    part = width // PIECES
    held = lambda size, kind: pltpu.VMEM((n_head, tok_dev, size), kind)
    cut = lambda kind: pltpu.VMEM((PIECES, n_head, tok_dev, part), kind)
    small = lambda kind: pltpu.VMEM((PIECES, 8, part), kind)
    whole = pltpu.VMEM((PIECES, STATE, part), F32)
    dma = pltpu.SemaphoreType.DMA
    many = dma((PIECES, STATE // CHUNK))
    return pl.pallas_call(
        functools.partial(block_kernel, n_ctx, n_head),
        out_shape=(
            jax.ShapeDtypeStruct(x_in.shape, BF16),
            jax.ShapeDtypeStruct(b_in.shape, BF16),
            jax.ShapeDtypeStruct(c_in.shape, BF16),
            jax.ShapeDtypeStruct(dt.shape, F32),
        ),
        in_specs=[pl.BlockSpec(memory_space=pltpu.VMEM)] * 6,
        out_specs=[pl.BlockSpec(memory_space=pltpu.VMEM)] * 4,
        scratch_shapes=[
            cut(BF16),
            cut(BF16),
            held(STATE, BF16),
            held(STATE, BF16),
            held(LANES, BF16),
            cut(BF16),
            held(STATE, F32),
            held(STATE, F32),
            held(LANES, BF16),
            held(STATE, F32),
            held(STATE, F32),
            held(LANES, BF16),
            dma((7 + 2 * PIECES,)),
            dma((7 + 2 * PIECES,)),
            pltpu.VMEM((PIECES, length + 8, part), F32),
            small(BF16),
            small(F32),
            small(F32),
            whole,
            whole,
            whole,
            small(F32),
            small(F32),
            whole,
            whole,
            whole,
            whole,
            pltpu.VMEM((length, length), F32),
            pltpu.VMEM((length, LANES), F32),
            pltpu.VMEM((PIECES, length, part), F32),
            dma((2, PIECES)),
            dma((2, PIECES)),
            dma((2, PIECES)),
            dma((2,)),
            many,
            many,
            many,
            many,
        ],
        compiler_params=pltpu.CompilerParams(
            vmem_limit_bytes=56 * 1024 * 1024, collective_id=0, has_side_effects=True
        ),
    )(x_in, grad_y, b_in, c_in, dt, params)


def solution(mesh):
    token = P(("ctx", "head"), None)
    in_specs = (token,) * 5 + (P(None, "head"), P("head"), P("head"), P("head"))
    return jax.shard_map(
        shards, mesh=mesh, in_specs=in_specs, out_specs=(token,) * 4, check_vma=False
    )
```

```python
import functools

import jax
import jax.numpy as jnp
from jax import lax
from jax.experimental import pallas as pl
from jax.experimental.pallas import tpu as pltpu
from jax.sharding import PartitionSpec as P

HEAD_DIM = 64
STATE = 256
GROUPS = 8
CONV = 4
LANES = 128
F32 = jnp.float32
BF16 = jnp.bfloat16
MESH = pl.DeviceIdType.MESH
PIECES = 2
CHUNK = 16 * PIECES


def nn(a, b):
    return lax.dot_general(a, b, (((1,), (0,)), ((), ())), preferred_element_type=F32)


def nt(a, b):
    return lax.dot_general(a, b, (((1,), (1,)), ((), ())), preferred_element_type=F32)


def split(value, pieces=2):
    parts = []
    for _ in range(pieces):
        part = value.astype(BF16)
        parts.append(part)
        value = value - part.astype(F32)
    return parts


def exact_by(dot, exact, wide):
    hi, lo = split(wide)
    return dot(exact, hi) + dot(exact, lo)


def wide_by(dot, wide, exact):
    hi, lo = split(wide)
    return dot(hi, exact) + dot(lo, exact)


def three(dot, left, right):
    lh, ll = split(left)
    rh, rl = split(right)
    return dot(lh, rh) + (dot(lh, rl) + dot(ll, rh))


def expand(cols, width, first=0):
    lane = lax.broadcasted_iota(jnp.int32, (cols.shape[0], LANES), 1)
    parts = [
        jnp.where(lane < HEAD_DIM, cols[:, h : h + 1], cols[:, h + 1 : h + 2])
        for h in range(first, first + width // HEAD_DIM, 2)
    ]
    return jnp.concatenate(parts, axis=1)


def segments(value, first=0):
    width = value.shape[1]
    row = lax.broadcasted_iota(jnp.int32, (width, LANES), 0)
    col = lax.broadcasted_iota(jnp.int32, (width, LANES), 1) - first
    pick = jnp.where(
        (row >= col * HEAD_DIM) & (row < (col + 1) * HEAD_DIM), 1.0, 0.0
    ).astype(BF16)
    return wide_by(nn, value, pick)


def triangle(length, lower):
    row = lax.broadcasted_iota(jnp.int32, (length, length), 0)
    col = lax.broadcasted_iota(jnp.int32, (length, length), 1)
    return row >= col if lower else row <= col


def convolve(x, par_ref, cols, ext):
    length = x.shape[0]
    ext[8 : 8 + length, :] = x
    conv = par_ref[4:5, cols] + par_ref[0:1, cols] * ext[5 : 5 + length, :]
    for k in range(1, CONV):
        conv = conv + par_ref[k : k + 1, cols] * ext[5 + k : 5 + k + length, :]
    return conv, 1.0 / (1.0 + jnp.exp(-conv))


def layout(pieces, part):
    boxes = [["dt", "b", "c", "x0"]] + [[] for _ in range(pieces - 1)]
    for p in range(pieces):
        if p + 1 < pieces:
            boxes[p].append("x%d" % (p + 1))
        boxes[p].append("dy%d" % p)
    sizes, plan = [], {}
    for box, names in enumerate(boxes):
        start = 0
        for name in names:
            size = {"dt": LANES, "b": STATE, "c": STATE}.get(name, part)
            plan[name] = (box, start, size, int(name[-1]) if name[-1].isdigit() else 0)
            start += size
        sizes.append(start)
    return sizes, plan


def flat(value):
    value = value.astype(F32)
    return value.reshape(value.shape[0] * value.shape[1], value.shape[2])


def block_kernel(
    n_ctx,
    n_head,
    x_ref,
    dy_ref,
    b_ref,
    c_ref,
    dt_ref,
    par_ref,
    gx_ref,
    gb_ref,
    gc_ref,
    gdt_ref,
    stage,
    got,
    gx_buf,
    gp_buf,
    gdt_buf,
    gp_all,
    gdt_all,
    head_send,
    head_recv,
    ext,
    edge,
    top_out,
    top_in,
    mine,
    other,
    sib_local,
    decay_own,
    decay_sib,
    chain_in,
    chain_out,
    sib_out,
    sib_in,
    gram_sum,
    cumul_sum,
    inner,
    edge_sems,
    top_sems,
    local_sems,
    decay_sems,
    chain_send,
    chain_recv,
    sib_send,
    sib_recv,
):
    pieces, length, part = ext.shape[0], ext.shape[1] - 8, ext.shape[2]
    width = pieces * part
    tok_dev = x_ref.shape[0]
    heads_dev = width // HEAD_DIM
    per_group = n_head // GROUPS
    per_tile = LANES // heads_dev
    head = lax.axis_index("head")
    me = lax.axis_index("ctx")
    core = lax.rem(me, 2)
    chip = lax.div(me, 2)
    chips = n_ctx // 2
    sign = 1 - 2 * core
    place = core * (chips - 1) + sign * chip
    sibling = me + sign
    per_piece = part // HEAD_DIM
    chunks = STATE // CHUNK
    pace = max(chips // pieces, 1)
    lag = lax.div(place + pace - 1, pace)
    late = place >= max(chips // 2 - 1, 1)
    early = jnp.logical_not(late)
    ahead = lax.rem(me + 2 * sign + n_ctx, n_ctx)
    following = lax.rem(me + 1, n_ctx)
    leading = lax.rem(me + n_ctx - 1, n_ctx)

    def remote(src, dst, sems, device, axis="ctx"):
        return pltpu.make_async_remote_copy(
            src_ref=src,
            dst_ref=dst,
            send_sem=sems[0],
            recv_sem=sems[1],
            device_id={axis: device},
            device_id_type=MESH,
        )

    plan = layout(pieces, part)[1]
    for to in range(n_head):
        for name, (box, start, size, p) in plan.items():
            if name == "dt":
                ref, first = dt_ref, to // per_tile * LANES
            elif name in ("b", "c"):
                ref, first = (b_ref if name == "b" else c_ref), to // per_group * STATE
            else:
                ref, first = (x_ref if name[0] == "x" else dy_ref), to * width + p * part
            stage[box][to, :, start : start + size] = ref[:, first : first + size]

    def piece_of(name):
        box, start, size, _ = plan[name]
        return flat(got[box][:, :, start : start + size])

    barrier = pltpu.get_barrier_semaphore()
    for by in (1, 2, n_ctx - 2, n_ctx - 1):
        pl.semaphore_signal(
            barrier,
            inc=1,
            device_id={"ctx": lax.rem(me + by, n_ctx)},
            device_id_type=MESH,
        )

    def greet(k, _):
        pl.semaphore_signal(
            barrier,
            inc=1,
            device_id={"head": lax.rem(head + k, n_head)},
            device_id_type=MESH,
        )
        return 0

    lax.fori_loop(1, n_head, greet, 0)
    pl.semaphore_wait(barrier, 3 + n_head)

    def scatter(kind, source, target):
        def step(k, _):
            to = lax.rem(head + k, n_head)
            remote(
                source(to), target, (head_send.at[kind], head_recv.at[kind]), to, "head"
            ).start()
            return 0

        lax.fori_loop(1, n_head, step, 0)
        pltpu.make_async_copy(source(head), target, head_recv.at[kind]).start()

    def arrived(kind, buffer):
        pltpu.make_async_copy(buffer, buffer, head_recv.at[kind]).wait()

    def sent(kind, buffer):
        pltpu.make_async_copy(buffer, buffer, head_send.at[kind]).wait()

    def lanes(ref, start, size):
        return ref.at[:, pl.ds(pl.multiple_of(start, LANES), size)]

    out_kind = pieces
    for p in range(pieces):
        scatter(p, lambda to: stage[p].at[to], got[p].at[head])

    @pl.when(place == 0)
    def _():
        chain_in[...] = jnp.zeros_like(chain_in)

    def edge_copy(p):
        box, start, size, _ = plan["x%d" % p]
        return remote(
            got[box].at[n_head - 1, tok_dev - 8 : tok_dev, start : start + size],
            edge.at[p],
            (edge_sems.at[0, p], edge_sems.at[1, p]),
            following,
        )

    def local_copy(p):
        return remote(
            other.at[p], sib_local.at[p], (local_sems.at[0, p], local_sems.at[1, p]), sibling
        )

    def top_copy(p):
        return remote(
            top_out.at[p], top_in.at[p], (top_sems.at[0, p], top_sems.at[1, p]), leading
        )

    def chain_copy(p, c):
        rows = pl.ds(pl.multiple_of(c * CHUNK, CHUNK), CHUNK)
        return remote(
            chain_out.at[p, rows, :],
            chain_in.at[p, rows, :],
            (chain_send.at[p, c], chain_recv.at[p, c]),
            ahead,
        )

    def sib_copy(p, c):
        rows = pl.ds(pl.multiple_of(c * CHUNK, CHUNK), CHUNK)
        return remote(
            sib_out.at[p, rows, :],
            sib_in.at[p, rows, :],
            (sib_send.at[p, c], sib_recv.at[p, c]),
            sibling,
        )

    lower = triangle(length, True)
    upper = triangle(length, False)
    lane = lax.broadcasted_iota(jnp.int32, (length, LANES), 1)
    arrived(0, got[0])
    edge_copy(0).start()
    if pieces > 1:
        edge_copy(1).start()
    shift = lax.rem(LANES - lax.rem(head, per_tile) * heads_dev, LANES)
    dt = jnp.where(lane < heads_dev, pltpu.roll(piece_of("dt"), shift, 1), 0.0)
    rate = par_ref[6:7, 0:LANES]
    cumul = -rate * nn(jnp.where(lower, 1.0, 0.0).astype(BF16), dt.astype(BF16))
    grow_cols = jnp.exp(cumul)
    tail_cols = jnp.exp(cumul[length - 1 : length, :] - cumul)
    for p in range(pieces):
        last = expand(grow_cols[length - 8 : length, :], part, p * per_piece)
        decay_own[p] = jnp.broadcast_to(last[7:8, :], (8, part))
    decay_copy = remote(
        decay_own, decay_sib, (decay_sems.at[0], decay_sems.at[1]), sibling
    )
    decay_copy.start()
    b32 = piece_of("b")
    c32 = piece_of("c")
    b16 = b32.astype(BF16)
    c16 = c32.astype(BF16)
    b_turned = b32.T.astype(BF16)
    c_turned = c32.T.astype(BF16)
    turned = cumul.T
    gram = nt(c16, b16)
    gram_turned = nt(b16, c16)
    gram_sum[...] = jnp.zeros_like(gram_sum)
    cumul_sum[...] = jnp.zeros_like(cumul_sum)
    first_core = core == 0

    def local(p):
        if p > 0:
            arrived(p, got[p])
        if 0 < p < pieces - 1:
            edge_copy(p + 1).start()
        cols = slice(p * part, (p + 1) * part)
        dy = piece_of("dy%d" % p)
        grow = expand(grow_cols, part, p * per_piece)
        tail = expand(tail_cols, part, p * per_piece)
        dt_wide = expand(dt, part, p * per_piece)
        dy_grown = dy * grow
        pull = exact_by(nn, c_turned, dy_grown)
        edge_copy(p).wait()
        ext[p, 0:8, :] = jnp.where(me > 0, edge[p].astype(F32), 0.0)
        conv, sig = convolve(piece_of("x%d" % p), par_ref, cols, ext.at[p])
        activ = conv * sig
        slope = sig * (1.0 + conv * (1.0 - sig))
        source = activ * dt_wide
        state = exact_by(nn, b_turned, source * tail)
        other[p] = jnp.where(first_core, pull, state)
        local_copy(p).start()
        mine[p] = jnp.where(first_core, state, pull)
        return (cols, dy, grow, tail, dt_wide, dy_grown, activ, slope, source)

    def chain(p):
        local_copy(p).wait_recv()

        def hop(c, _):
            rows = pl.ds(pl.multiple_of(c * CHUNK, CHUNK), CHUNK)

            @pl.when(place > 0)
            def _():
                chain_copy(p, c).wait_recv()

            here = decay_own[p, 0:1, :] * chain_in[p, rows, :] + mine[p, rows, :]
            chain_out[p, rows, :] = decay_sib[p, 0:1, :] * here + sib_local[p, rows, :]

            @pl.when(place < chips - 1)
            def _():
                chain_copy(p, c).start()

            sib_out[p, rows, :] = here
            sib_copy(p, c).start()
            return 0

        lax.fori_loop(0, chunks, hop, 0)

    def within(p):
        dy, source = held[p][1], held[p][8]
        g_gram = gram_sum[...]
        g_cumul = cumul_sum[...]
        for pair in range(part // LANES):
            at = slice(pair * LANES, (pair + 1) * LANES)
            src_hi, src_lo = split(source[:, at])
            dy16 = dy[:, at].astype(BF16)
            halves = []
            for side in range(2):
                h = p * per_piece + 2 * pair + side
                own = lane < HEAD_DIM if side == 0 else lane >= HEAD_DIM
                dy_own = jnp.where(own, dy[:, at], 0.0).astype(BF16)
                col = cumul[:, h : h + 1]
                row = turned[h : h + 1, :]
                decay = jnp.where(lower, jnp.exp(jnp.minimum(col - row, 0.0)), 0.0)
                inside = decay * (nt(dy_own, src_hi) + nt(dy_own, src_lo))
                g_gram = g_gram + inside
                g_cumul = g_cumul + jnp.where(
                    lane == h, jnp.sum(inside * gram, axis=1, keepdims=True), 0.0
                )
                mixing = gram_turned * jnp.where(
                    upper, jnp.exp(jnp.minimum(row - col, 0.0)), 0.0
                )
                halves.append(wide_by(nn, mixing, dy16))
            inner[p, :, at] = jnp.where(lane < HEAD_DIM, halves[0], halves[1])
        gram_sum[...] = g_gram
        cumul_sum[...] = g_cumul

    held = []
    for step in range(pieces):
        held.append(local(step))
        if step == 0:
            decay_copy.wait()

        @pl.when(step >= lag)
        def _():
            chain(step - lag)

        if step + 1 < pieces:
            within(step)

    @pl.when(late)
    def _():
        within(pieces - 1)

    for j in range(1, pieces):

        @pl.when(early & (lag >= j))
        def _():
            chain(pieces - 1 - lag + j)

    @pl.when(early)
    def _():
        within(pieces - 1)

    def by_token(value):
        return value.reshape(n_head, tok_dev, value.shape[1])

    def finish(p):
        cols = held[p][0]
        top_copy(p).wait()
        ext[p, length : length + 8, :] = jnp.where(me < n_ctx - 1, top_in[p], 0.0)
        g_x = par_ref[3:4, cols] * ext[p, 0:length, :]
        for k in range(CONV - 1):
            back = CONV - 1 - k
            g_x = g_x + par_ref[k : k + 1, cols] * ext[p, back : back + length, :]
        gx_buf[p] = by_token(g_x).astype(BF16)
        scatter(
            out_kind + 2,
            lambda to: gx_buf.at[p, to],
            lanes(gx_ref, head * width + p * part, part),
        )

    g_gram = gram_sum[...]
    g_b = wide_by(nn, g_gram.T, c16)
    g_c = wide_by(nn, g_gram, b16)
    direct = jnp.zeros((length, LANES), F32)
    g_cumul = cumul_sum[...]
    total = jnp.zeros((16, LANES), F32)
    for p in range(pieces):

        @pl.when(late & (lag > pieces - 1 - p))
        def _():
            chain(p)

        lax.fori_loop(0, chunks, lambda c, _: (sib_copy(p, c).wait_recv(), 0)[1], 0)
        cols, dy, grow, tail, dt_wide, dy_grown, activ, slope, source = held[p]
        state = jnp.where(first_core, chain_in[p], sib_in[p])
        pull = jnp.where(first_core, sib_in[p], chain_in[p])
        pulled = tail * exact_by(nn, b16, pull)
        g_source = inner[p] + pulled
        skip = expand(par_ref[7:8, 0:LANES], part, p * per_piece)
        g_conv = (dt_wide * g_source + skip * dy) * slope
        ext[p, 0:length, :] = g_conv
        top_out[p] = g_conv[0:8, :]
        top_copy(p).start()
        g_b = g_b + three(nt, source * tail, pull)
        g_c = g_c + three(nt, dy_grown, state)
        if p + 1 == pieces:
            gp_buf[:, :, 0:STATE] = by_token(g_b)
            gp_buf[:, :, STATE : 2 * STATE] = by_token(g_c)
            scatter(out_kind, lambda to: gp_buf.at[to], gp_all.at[head])
        first = p * per_piece
        direct = direct + segments(activ * g_source, first)
        g_cumul = g_cumul + segments(dy_grown * exact_by(nn, c16, state), first)
        carried = jnp.sum(source * pulled, axis=0, keepdims=True) + grow[
            length - 1 : length, :
        ] * jnp.sum(state * pull, axis=0, keepdims=True)
        total = total + segments(jnp.broadcast_to(carried, (16, part)), first)
        if p > 0:
            finish(p - 1)
    finish(pieces - 1)

    after = jnp.where(upper, 1.0, 0.0).astype(BF16)
    terms = split(g_cumul - dt * direct, 3)
    later = nn(after, terms[0]) + (nn(after, terms[1]) + nn(after, terms[2]))
    g_dt = direct - rate * (later + total[0:1, :])
    merged = jnp.zeros((length, LANES), F32)
    for j, term in enumerate(split(g_dt, 3)):
        term = term.astype(F32)
        merged = merged + (pltpu.roll(term, j * heads_dev, 1) if j else term)
    gdt_buf[...] = by_token(merged).astype(BF16)
    scatter(out_kind + 1, lambda to: gdt_buf.at[to], gdt_all.at[head])

    arrived(out_kind, gp_all)
    for g in range(GROUPS):
        summed = gp_all[g * per_group]
        for j in range(1, per_group):
            summed = summed + gp_all[g * per_group + j]
        summed = summed.astype(BF16)
        gb_ref[:, g * STATE : (g + 1) * STATE] = summed[:, 0:STATE]
        gc_ref[:, g * STATE : (g + 1) * STATE] = summed[:, STATE : 2 * STATE]
    arrived(out_kind + 1, gdt_all)
    own = lax.broadcasted_iota(jnp.int32, (tok_dev, LANES), 1) < heads_dev
    for tile in range(n_head // per_tile):
        summed = jnp.zeros((tok_dev, LANES), F32)
        for j in range(per_tile):
            value = gdt_all[tile * per_tile + j].astype(F32)
            value = (
                value
                + pltpu.roll(value, LANES - heads_dev, 1)
                + pltpu.roll(value, LANES - 2 * heads_dev, 1)
            )
            value = jnp.where(own, value, 0.0)
            summed = summed + (pltpu.roll(value, j * heads_dev, 1) if j else value)
        gdt_ref[:, tile * LANES : (tile + 1) * LANES] = summed
    arrived(out_kind + 2, gx_ref)

    for p in range(pieces):
        sent(p, stage[p].at[0 : n_head - 1])
        local_copy(p).wait_send()

        def drain(c, _):
            @pl.when(place < chips - 1)
            def _():
                chain_copy(p, c).wait_send()

            sib_copy(p, c).wait_send()
            return 0

        lax.fori_loop(0, chunks, drain, 0)
    sent(out_kind, gp_buf.at[0 : n_head - 1])
    sent(out_kind + 1, gdt_buf.at[0 : n_head - 1])
    sent(out_kind + 2, gx_buf.at[:, 0 : n_head - 1])


def shards(x_in, grad_y, b_in, c_in, dt, conv_weight, conv_bias, decay_rate, skip):
    n_head = lax.axis_size("head")
    n_ctx = lax.axis_size("ctx")
    per_group = n_head // GROUPS
    tok_dev = x_in.shape[0]
    heads_dev = decay_rate.shape[0]
    width = heads_dev * HEAD_DIM
    length = tok_dev * n_head

    wide = lambda value: jnp.pad(value[None, :], ((0, 0), (0, width - heads_dev)))
    params = jnp.concatenate(
        [conv_weight, conv_bias[None, :], conv_bias[None, :], wide(decay_rate), wide(skip)], axis=0
    )
    part = width // PIECES
    sizes = layout(PIECES, part)[0]
    held = lambda size, kind: pltpu.VMEM((n_head, tok_dev, size), kind)
    cut = lambda kind: pltpu.VMEM((PIECES, n_head, tok_dev, part), kind)
    small = lambda kind: pltpu.VMEM((PIECES, 8, part), kind)
    whole = pltpu.VMEM((PIECES, STATE, part), F32)
    dma = pltpu.SemaphoreType.DMA
    many = dma((PIECES, STATE // CHUNK))
    return pl.pallas_call(
        functools.partial(block_kernel, n_ctx, n_head),
        out_shape=(
            jax.ShapeDtypeStruct(x_in.shape, BF16),
            jax.ShapeDtypeStruct(b_in.shape, BF16),
            jax.ShapeDtypeStruct(c_in.shape, BF16),
            jax.ShapeDtypeStruct(dt.shape, F32),
        ),
        in_specs=[pl.BlockSpec(memory_space=pltpu.VMEM)] * 6,
        out_specs=[pl.BlockSpec(memory_space=pltpu.VMEM)] * 4,
        scratch_shapes=[
            [held(size, BF16) for size in sizes],
            [held(size, BF16) for size in sizes],
            cut(BF16),
            held(2 * STATE, F32),
            held(LANES, BF16),
            held(2 * STATE, F32),
            held(LANES, BF16),
            dma((3 + PIECES,)),
            dma((3 + PIECES,)),
            pltpu.VMEM((PIECES, length + 8, part), F32),
            small(BF16),
            small(F32),
            small(F32),
            whole,
            whole,
            whole,
            small(F32),
            small(F32),
            whole,
            whole,
            whole,
            whole,
            pltpu.VMEM((length, length), F32),
            pltpu.VMEM((length, LANES), F32),
            pltpu.VMEM((PIECES, length, part), F32),
            dma((2, PIECES)),
            dma((2, PIECES)),
            dma((2, PIECES)),
            dma((2,)),
            many,
            many,
            many,
            many,
        ],
        compiler_params=pltpu.CompilerParams(
            vmem_limit_bytes=56 * 1024 * 1024, collective_id=0, has_side_effects=True
        ),
    )(x_in, grad_y, b_in, c_in, dt, params)


def solution(mesh):
    token = P(("ctx", "head"), None)
    in_specs = (token,) * 5 + (P(None, "head"), P("head"), P("head"), P("head"))
    return jax.shard_map(
        shards, mesh=mesh, in_specs=in_specs, out_specs=(token,) * 4, check_vma=False
    )
```

```python
import functools

import jax
import jax.numpy as jnp
from jax import lax
from jax.experimental import pallas as pl
from jax.experimental.pallas import tpu as pltpu
from jax.sharding import PartitionSpec as P

HEAD_DIM = 64
STATE = 256
GROUPS = 8
CONV = 4
LANES = 128
F32 = jnp.float32
BF16 = jnp.bfloat16
MESH = pl.DeviceIdType.MESH
CHUNK = 16


def nn(a, b):
    return lax.dot_general(a, b, (((1,), (0,)), ((), ())), preferred_element_type=F32)


def nt(a, b):
    return lax.dot_general(a, b, (((1,), (1,)), ((), ())), preferred_element_type=F32)


def split(value, pieces=2):
    parts = []
    for _ in range(pieces):
        part = value.astype(BF16)
        parts.append(part)
        value = value - part.astype(F32)
    return parts


def exact_by(dot, exact, wide):
    hi, lo = split(wide)
    return dot(exact, hi) + dot(exact, lo)


def wide_by(dot, wide, exact):
    hi, lo = split(wide)
    return dot(hi, exact) + dot(lo, exact)


def three(dot, left, right):
    lh, ll = split(left)
    rh, rl = split(right)
    return dot(lh, rh) + (dot(lh, rl) + dot(ll, rh))


def expand(cols, width):
    lane = lax.broadcasted_iota(jnp.int32, (cols.shape[0], LANES), 1)
    parts = [
        jnp.where(lane < HEAD_DIM, cols[:, h : h + 1], cols[:, h + 1 : h + 2])
        for h in range(0, width // HEAD_DIM, 2)
    ]
    return jnp.concatenate(parts, axis=1)


def segments(value):
    width = value.shape[1]
    row = lax.broadcasted_iota(jnp.int32, (width, LANES), 0)
    col = lax.broadcasted_iota(jnp.int32, (width, LANES), 1)
    pick = jnp.where(
        (row >= col * HEAD_DIM) & (row < (col + 1) * HEAD_DIM), 1.0, 0.0
    ).astype(BF16)
    return wide_by(nn, value, pick)


def triangle(length, lower):
    row = lax.broadcasted_iota(jnp.int32, (length, length), 0)
    col = lax.broadcasted_iota(jnp.int32, (length, length), 1)
    return row >= col if lower else row <= col


def convolve(x, par_ref, ext):
    length = x.shape[0]
    ext[8 : 8 + length, :] = x
    conv = par_ref[4:5, :] + par_ref[0:1, :] * ext[5 : 5 + length, :]
    for k in range(1, CONV):
        conv = conv + par_ref[k : k + 1, :] * ext[5 + k : 5 + k + length, :]
    return conv, 1.0 / (1.0 + jnp.exp(-conv))


def flat(ref):
    value = ref[...].astype(F32)
    return value.reshape(value.shape[0] * value.shape[1], value.shape[2])


def block_kernel(
    n_ctx,
    n_head,
    x_ref,
    dy_ref,
    b_ref,
    c_ref,
    dt_ref,
    weight_ref,
    bias_ref,
    rate_ref,
    skip_ref,
    gx_ref,
    gb_ref,
    gc_ref,
    gdt_ref,
    x_buf,
    dy_buf,
    b_buf,
    c_buf,
    dt_buf,
    gx_buf,
    gb_buf,
    gc_buf,
    gdt_buf,
    gb_all,
    gc_all,
    gdt_all,
    par_ref,
    head_send,
    head_recv,
    ext,
    edge,
    top_out,
    top_in,
    mine,
    other,
    sib_local,
    decay_own,
    decay_sib,
    chain_in,
    chain_out,
    sib_out,
    sib_in,
    gram_sum,
    cumul_sum,
    inner,
    edge_sems,
    top_sems,
    local_sems,
    decay_sems,
    chain_send,
    chain_recv,
    sib_send,
    sib_recv,
):
    length, width = ext.shape[0] - 8, ext.shape[1]
    tok_dev = x_ref.shape[0]
    heads_dev = width // HEAD_DIM
    per_group = n_head // GROUPS
    per_tile = LANES // heads_dev
    head = lax.axis_index("head")
    me = lax.axis_index("ctx")
    core = lax.rem(me, 2)
    chip = lax.div(me, 2)
    chips = n_ctx // 2
    sign = 1 - 2 * core
    place = core * (chips - 1) + sign * chip
    sibling = me + sign
    ahead = lax.rem(me + 2 * sign + n_ctx, n_ctx)
    following = lax.rem(me + 1, n_ctx)
    leading = lax.rem(me + n_ctx - 1, n_ctx)

    def remote(src, dst, sems, device, axis="ctx"):
        return pltpu.make_async_remote_copy(
            src_ref=src,
            dst_ref=dst,
            send_sem=sems[0],
            recv_sem=sems[1],
            device_id={axis: device},
            device_id_type=MESH,
        )

    par_ref[0:CONV, :] = weight_ref[...]
    par_ref[CONV : CONV + 1, :] = bias_ref[...]
    par_ref[5:8, :] = jnp.zeros((3, width), F32)
    par_ref[6:7, 0:heads_dev] = rate_ref[...]
    par_ref[7:8, 0:heads_dev] = skip_ref[...]

    barrier = pltpu.get_barrier_semaphore()
    for by in (1, 2, n_ctx - 2, n_ctx - 1):
        pl.semaphore_signal(
            barrier,
            inc=1,
            device_id={"ctx": lax.rem(me + by, n_ctx)},
            device_id_type=MESH,
        )

    def greet(k, _):
        pl.semaphore_signal(
            barrier,
            inc=1,
            device_id={"head": lax.rem(head + k, n_head)},
            device_id_type=MESH,
        )
        return 0

    lax.fori_loop(1, n_head, greet, 0)
    pl.semaphore_wait(barrier, 3 + n_head)

    def scatter(kind, source, target):
        def step(k, _):
            to = lax.rem(head + k, n_head)
            remote(
                source(to), target, (head_send.at[kind], head_recv.at[kind]), to, "head"
            ).start()
            return 0

        lax.fori_loop(1, n_head, step, 0)
        pltpu.make_async_copy(source(head), target, head_recv.at[kind]).start()

    def arrived(kind, buffer):
        pltpu.make_async_copy(buffer, buffer, head_recv.at[kind]).wait()

    def sent(kind, buffer):
        part = buffer.at[0 : n_head - 1]
        pltpu.make_async_copy(part, part, head_send.at[kind]).wait()

    def lanes(ref, start, size):
        return ref.at[:, pl.ds(pl.multiple_of(start, LANES), size)]

    scatter(0, lambda to: lanes(b_ref, lax.div(to, per_group) * STATE, STATE), b_buf.at[head])
    scatter(1, lambda to: lanes(c_ref, lax.div(to, per_group) * STATE, STATE), c_buf.at[head])
    scatter(2, lambda to: lanes(dt_ref, lax.div(to, per_tile) * LANES, LANES), dt_buf.at[head])
    scatter(3, lambda to: lanes(x_ref, to * width, width), x_buf.at[head])
    scatter(4, lambda to: lanes(dy_ref, to * width, width), dy_buf.at[head])

    lower = triangle(length, True)
    upper = triangle(length, False)
    lane = lax.broadcasted_iota(jnp.int32, (length, LANES), 1)
    arrived(0, b_buf)
    arrived(1, c_buf)
    arrived(2, dt_buf)
    shift = lax.rem(LANES - lax.rem(head, per_tile) * heads_dev, LANES)
    dt = jnp.where(lane < heads_dev, pltpu.roll(flat(dt_buf), shift, 1), 0.0)
    rate = par_ref[6:7, 0:LANES]
    cumul = -rate * nn(jnp.where(lower, 1.0, 0.0).astype(BF16), dt.astype(BF16))
    grow = expand(jnp.exp(cumul), width)
    tail = expand(jnp.exp(cumul[length - 1 : length, :] - cumul), width)
    dt_wide = expand(dt, width)
    b32 = flat(b_buf)
    c32 = flat(c_buf)
    b16 = b32.astype(BF16)
    c16 = c32.astype(BF16)
    b_turned = b32.T.astype(BF16)
    c_turned = c32.T.astype(BF16)
    decay_own[...] = jnp.broadcast_to(grow[length - 1 : length, :], (8, width))
    decay_copy = remote(
        decay_own, decay_sib, (decay_sems.at[0], decay_sems.at[1]), sibling
    )
    decay_copy.start()
    arrived(3, x_buf)
    edge_copy = remote(
        x_buf.at[n_head - 1, tok_dev - 8 : tok_dev, :],
        edge,
        (edge_sems.at[0], edge_sems.at[1]),
        following,
    )
    edge_copy.start()
    arrived(4, dy_buf)
    dy = flat(dy_buf)
    dy16 = dy.astype(BF16)
    dy_grown = dy * grow
    pull = exact_by(nn, c_turned, dy_grown)

    edge_copy.wait()
    ext[0:8, :] = jnp.where(me > 0, edge[...].astype(F32), 0.0)
    conv, sig = convolve(flat(x_buf), par_ref, ext)
    activ = conv * sig
    slope = sig * (1.0 + conv * (1.0 - sig))
    source = activ * dt_wide
    state = exact_by(nn, b_turned, source * tail)
    first_core = core == 0
    other[...] = jnp.where(first_core, pull, state)
    mine[...] = jnp.where(first_core, state, pull)
    local_copy = remote(
        other, sib_local, (local_sems.at[0], local_sems.at[1]), sibling
    )
    local_copy.start()

    def within():
        turned = cumul.T
        gram = nt(c16, b16)
        gram_turned = nt(b16, c16)
        g_gram = jnp.zeros((length, length), F32)
        g_cumul = jnp.zeros((length, LANES), F32)
        for pair in range(width // LANES):
            at = slice(pair * LANES, (pair + 1) * LANES)
            src_hi, src_lo = split(source[:, at])
            halves = []
            for side in range(2):
                h = 2 * pair + side
                own = lane < HEAD_DIM if side == 0 else lane >= HEAD_DIM
                dy_own = jnp.where(own, dy[:, at], 0.0).astype(BF16)
                col = cumul[:, h : h + 1]
                row = turned[h : h + 1, :]
                decay = jnp.where(lower, jnp.exp(jnp.minimum(col - row, 0.0)), 0.0)
                inside = decay * (nt(dy_own, src_hi) + nt(dy_own, src_lo))
                g_gram = g_gram + inside
                g_cumul = g_cumul + jnp.where(
                    lane == h, jnp.sum(inside * gram, axis=1, keepdims=True), 0.0
                )
                mixing = gram_turned * jnp.where(
                    upper, jnp.exp(jnp.minimum(row - col, 0.0)), 0.0
                )
                halves.append(wide_by(nn, mixing, dy16[:, at]))
            inner[:, at] = jnp.where(lane < HEAD_DIM, halves[0], halves[1])
        gram_sum[...] = g_gram
        cumul_sum[...] = g_cumul

    late = place >= (chips + 1) // 2

    @pl.when(place == 0)
    def _():
        chain_in[...] = jnp.zeros_like(chain_in)

    decay_copy.wait()
    local_copy.wait()

    @pl.when(late)
    def _():
        within()

    def chain_copy(c):
        rows = pl.ds(pl.multiple_of(c * CHUNK, CHUNK), CHUNK)
        return remote(
            chain_out.at[rows, :],
            chain_in.at[rows, :],
            (chain_send.at[c], chain_recv.at[c]),
            ahead,
        )

    def sib_copy(c):
        rows = pl.ds(pl.multiple_of(c * CHUNK, CHUNK), CHUNK)
        return remote(
            sib_out.at[rows, :],
            sib_in.at[rows, :],
            (sib_send.at[c], sib_recv.at[c]),
            sibling,
        )

    def hop(c, _):
        rows = pl.ds(pl.multiple_of(c * CHUNK, CHUNK), CHUNK)

        @pl.when(place > 0)
        def _():
            chain_copy(c).wait_recv()

        here = decay_own[0:1, :] * chain_in[rows, :] + mine[rows, :]
        chain_out[rows, :] = decay_sib[0:1, :] * here + sib_local[rows, :]

        @pl.when(place < chips - 1)
        def _():
            chain_copy(c).start()

        sib_out[rows, :] = here
        sib_copy(c).start()
        return 0

    chunks = STATE // CHUNK
    lax.fori_loop(0, chunks, hop, 0)

    @pl.when(jnp.logical_not(late))
    def _():
        within()

    def drain(c, _):
        @pl.when(place < chips - 1)
        def _():
            chain_copy(c).wait_send()

        sib_copy(c).wait()
        return 0

    lax.fori_loop(0, chunks, drain, 0)

    state = jnp.where(first_core, chain_in[...], sib_in[...])
    pull = jnp.where(first_core, sib_in[...], chain_in[...])
    pulled = tail * exact_by(nn, b16, pull)
    g_source = inner[...] + pulled
    g_conv = (dt_wide * g_source + expand(par_ref[7:8, 0:LANES], width) * dy) * slope
    ext[0:length, :] = g_conv
    top_out[...] = g_conv[0:8, :]
    top_copy = remote(top_out, top_in, (top_sems.at[0], top_sems.at[1]), leading)
    top_copy.start()

    def by_token(value):
        return value.reshape(n_head, tok_dev, value.shape[1])

    g_gram = gram_sum[...]
    gb_buf[...] = by_token(
        wide_by(nn, g_gram.T, c16) + three(nt, source * tail, pull)
    )
    scatter(5, lambda to: gb_buf.at[to], gb_all.at[head])
    gc_buf[...] = by_token(wide_by(nn, g_gram, b16) + three(nt, dy_grown, state))
    scatter(6, lambda to: gc_buf.at[to], gc_all.at[head])

    top_copy.wait()
    ext[length : length + 8, :] = jnp.where(me < n_ctx - 1, top_in[...], 0.0)
    g_x = par_ref[3:4, :] * g_conv
    for k in range(CONV - 1):
        g_x = g_x + par_ref[k : k + 1, :] * ext[CONV - 1 - k : CONV - 1 - k + length, :]
    gx_buf[...] = by_token(g_x).astype(BF16)
    scatter(7, lambda to: gx_buf.at[to], lanes(gx_ref, head * width, width))

    direct = segments(activ * g_source)
    g_cumul = (
        cumul_sum[...] + segments(dy_grown * exact_by(nn, c16, state)) - dt * direct
    )
    carried = jnp.sum(source * pulled, axis=0, keepdims=True) + grow[
        length - 1 : length, :
    ] * jnp.sum(state * pull, axis=0, keepdims=True)
    carried = segments(jnp.broadcast_to(carried, (16, width)))[0:1, :]
    after = jnp.where(upper, 1.0, 0.0).astype(BF16)
    pieces = split(g_cumul, 3)
    later = nn(after, pieces[0]) + (nn(after, pieces[1]) + nn(after, pieces[2]))
    g_dt = direct - rate * (later + carried)
    merged = jnp.zeros((length, LANES), F32)
    for j, part in enumerate(split(g_dt, 3)):
        part = part.astype(F32)
        merged = merged + (pltpu.roll(part, j * heads_dev, 1) if j else part)
    gdt_buf[...] = by_token(merged).astype(BF16)
    scatter(8, lambda to: gdt_buf.at[to], gdt_all.at[head])

    for kind, buffer, result in ((5, gb_all, gb_ref), (6, gc_all, gc_ref)):
        arrived(kind, buffer)
        for g in range(GROUPS):
            summed = buffer[g * per_group]
            for j in range(1, per_group):
                summed = summed + buffer[g * per_group + j]
            result[:, g * STATE : (g + 1) * STATE] = summed.astype(BF16)
    arrived(8, gdt_all)
    own = lax.broadcasted_iota(jnp.int32, (tok_dev, LANES), 1) < heads_dev
    for tile in range(n_head // per_tile):
        summed = jnp.zeros((tok_dev, LANES), F32)
        for j in range(per_tile):
            value = gdt_all[tile * per_tile + j].astype(F32)
            value = (
                value
                + pltpu.roll(value, LANES - heads_dev, 1)
                + pltpu.roll(value, LANES - 2 * heads_dev, 1)
            )
            value = jnp.where(own, value, 0.0)
            summed = summed + (pltpu.roll(value, j * heads_dev, 1) if j else value)
        gdt_ref[:, tile * LANES : (tile + 1) * LANES] = summed
    arrived(7, gx_ref)
    for kind, buffer in enumerate(
        (b_buf, c_buf, dt_buf, x_buf, dy_buf, gb_buf, gc_buf, gx_buf, gdt_buf)
    ):
        sent(kind, buffer)


def shards(x_in, grad_y, b_in, c_in, dt, conv_weight, conv_bias, decay_rate, skip):
    n_head = lax.axis_size("head")
    n_ctx = lax.axis_size("ctx")
    per_group = n_head // GROUPS
    tok_dev = x_in.shape[0]
    heads_dev = decay_rate.shape[0]
    width = heads_dev * HEAD_DIM
    length = tok_dev * n_head

    whole = pltpu.VMEM((STATE, width), F32)
    small = pltpu.VMEM((8, width), F32)
    held = lambda size, kind: pltpu.VMEM((n_head, tok_dev, size), kind)
    pair = pltpu.SemaphoreType.DMA((2,))
    many = pltpu.SemaphoreType.DMA((STATE // CHUNK,))
    return pl.pallas_call(
        functools.partial(block_kernel, n_ctx, n_head),
        out_shape=(
            jax.ShapeDtypeStruct(x_in.shape, BF16),
            jax.ShapeDtypeStruct(b_in.shape, BF16),
            jax.ShapeDtypeStruct(c_in.shape, BF16),
            jax.ShapeDtypeStruct(dt.shape, F32),
        ),
        in_specs=[pl.BlockSpec(memory_space=pltpu.VMEM)] * 9,
        out_specs=[pl.BlockSpec(memory_space=pltpu.VMEM)] * 4,
        scratch_shapes=[
            held(width, BF16),
            held(width, BF16),
            held(STATE, BF16),
            held(STATE, BF16),
            held(LANES, BF16),
            held(width, BF16),
            held(STATE, F32),
            held(STATE, F32),
            held(LANES, BF16),
            held(STATE, F32),
            held(STATE, F32),
            held(LANES, BF16),
            small,
            pltpu.SemaphoreType.DMA((9,)),
            pltpu.SemaphoreType.DMA((9,)),
            pltpu.VMEM((length + 8, width), F32),
            pltpu.VMEM((8, width), BF16),
            small,
            small,
            whole,
            whole,
            whole,
            small,
            small,
            whole,
            whole,
            whole,
            whole,
            pltpu.VMEM((length, length), F32),
            pltpu.VMEM((length, LANES), F32),
            pltpu.VMEM((length, width), F32),
            pair,
            pair,
            pair,
            pair,
            many,
            many,
            many,
            many,
        ],
        compiler_params=pltpu.CompilerParams(
            vmem_limit_bytes=56 * 1024 * 1024, collective_id=0, has_side_effects=True
        ),
    )(
        x_in,
        grad_y,
        b_in,
        c_in,
        dt,
        conv_weight,
        conv_bias[None, :],
        decay_rate[None, :],
        skip[None, :],
    )


def solution(mesh):
    token = P(("ctx", "head"), None)
    in_specs = (token,) * 5 + (P(None, "head"), P("head"), P("head"), P("head"))
    return jax.shard_map(
        shards, mesh=mesh, in_specs=in_specs, out_specs=(token,) * 4, check_vma=False
    )
```

```python
import functools

import jax
import jax.numpy as jnp
from jax import lax
from jax.experimental import pallas as pl
from jax.experimental.pallas import tpu as pltpu
from jax.sharding import PartitionSpec as P

HEAD_DIM = 64
STATE = 256
GROUPS = 8
CONV = 4
LANES = 128
F32 = jnp.float32
BF16 = jnp.bfloat16
MESH = pl.DeviceIdType.MESH
CHUNK = 8


def nn(a, b):
    return lax.dot_general(a, b, (((1,), (0,)), ((), ())), preferred_element_type=F32)


def nt(a, b):
    return lax.dot_general(a, b, (((1,), (1,)), ((), ())), preferred_element_type=F32)


def split(value, pieces=2):
    parts = []
    for _ in range(pieces):
        part = value.astype(BF16)
        parts.append(part)
        value = value - part.astype(F32)
    return parts


def exact_by(dot, exact, wide):
    hi, lo = split(wide)
    return dot(exact, hi) + dot(exact, lo)


def wide_by(dot, wide, exact):
    hi, lo = split(wide)
    return dot(hi, exact) + dot(lo, exact)


def three(dot, left, right):
    lh, ll = split(left)
    rh, rl = split(right)
    return dot(lh, rh) + (dot(lh, rl) + dot(ll, rh))


def expand(cols, width):
    lane = lax.broadcasted_iota(jnp.int32, (cols.shape[0], LANES), 1)
    parts = [
        jnp.where(lane < HEAD_DIM, cols[:, h : h + 1], cols[:, h + 1 : h + 2])
        for h in range(0, width // HEAD_DIM, 2)
    ]
    return jnp.concatenate(parts, axis=1)


def segments(value):
    width = value.shape[1]
    row = lax.broadcasted_iota(jnp.int32, (width, LANES), 0)
    col = lax.broadcasted_iota(jnp.int32, (width, LANES), 1)
    pick = jnp.where(
        (row >= col * HEAD_DIM) & (row < (col + 1) * HEAD_DIM), 1.0, 0.0
    ).astype(BF16)
    return wide_by(nn, value, pick)


def triangle(length, lower):
    row = lax.broadcasted_iota(jnp.int32, (length, length), 0)
    col = lax.broadcasted_iota(jnp.int32, (length, length), 1)
    return row >= col if lower else row <= col


def convolve(x, par_ref, ext):
    length = x.shape[0]
    ext[8 : 8 + length, :] = x
    conv = par_ref[4:5, :] + par_ref[0:1, :] * ext[5 : 5 + length, :]
    for k in range(1, CONV):
        conv = conv + par_ref[k : k + 1, :] * ext[5 + k : 5 + k + length, :]
    return conv, 1.0 / (1.0 + jnp.exp(-conv))


def flat(ref):
    value = ref[...].astype(F32)
    return value.reshape(value.shape[0] * value.shape[1], value.shape[2])


def block_kernel(
    n_ctx,
    n_head,
    x_ref,
    dy_ref,
    b_ref,
    c_ref,
    dt_ref,
    weight_ref,
    bias_ref,
    rate_ref,
    skip_ref,
    gx_ref,
    gb_ref,
    gc_ref,
    gdt_ref,
    x_buf,
    dy_buf,
    b_buf,
    c_buf,
    dt_buf,
    gx_buf,
    gb_buf,
    gc_buf,
    gdt_buf,
    gb_all,
    gc_all,
    gdt_all,
    par_ref,
    head_send,
    head_recv,
    ext,
    edge,
    top_out,
    top_in,
    mine,
    other,
    sib_local,
    decay_own,
    decay_sib,
    chain_in,
    chain_out,
    sib_out,
    sib_in,
    gram_sum,
    cumul_sum,
    inner,
    edge_sems,
    top_sems,
    local_sems,
    decay_sems,
    chain_send,
    chain_recv,
    sib_send,
    sib_recv,
):
    length, width = ext.shape[0] - 8, ext.shape[1]
    tok_dev = x_ref.shape[0]
    heads_dev = width // HEAD_DIM
    per_group = n_head // GROUPS
    per_tile = LANES // heads_dev
    head = lax.axis_index("head")
    me = lax.axis_index("ctx")
    core = lax.rem(me, 2)
    chip = lax.div(me, 2)
    chips = n_ctx // 2
    sign = 1 - 2 * core
    place = core * (chips - 1) + sign * chip
    sibling = me + sign
    ahead = lax.rem(me + 2 * sign + n_ctx, n_ctx)
    following = lax.rem(me + 1, n_ctx)
    leading = lax.rem(me + n_ctx - 1, n_ctx)

    def remote(src, dst, sems, device, axis="ctx"):
        return pltpu.make_async_remote_copy(
            src_ref=src,
            dst_ref=dst,
            send_sem=sems[0],
            recv_sem=sems[1],
            device_id={axis: device},
            device_id_type=MESH,
        )

    par_ref[0:CONV, :] = weight_ref[...]
    par_ref[CONV : CONV + 1, :] = bias_ref[...]
    par_ref[5:8, :] = jnp.zeros((3, width), F32)
    par_ref[6:7, 0:heads_dev] = rate_ref[...]
    par_ref[7:8, 0:heads_dev] = skip_ref[...]

    barrier = pltpu.get_barrier_semaphore()
    for by in (1, 2, n_ctx - 2, n_ctx - 1):
        pl.semaphore_signal(
            barrier,
            inc=1,
            device_id={"ctx": lax.rem(me + by, n_ctx)},
            device_id_type=MESH,
        )

    def greet(k, _):
        pl.semaphore_signal(
            barrier,
            inc=1,
            device_id={"head": lax.rem(head + k, n_head)},
            device_id_type=MESH,
        )
        return 0

    lax.fori_loop(1, n_head, greet, 0)
    pl.semaphore_wait(barrier, 3 + n_head)

    def scatter(kind, source, target):
        def step(k, _):
            to = lax.rem(head + k, n_head)
            remote(
                source(to), target, (head_send.at[kind], head_recv.at[kind]), to, "head"
            ).start()
            return 0

        lax.fori_loop(1, n_head, step, 0)
        pltpu.make_async_copy(source(head), target, head_recv.at[kind]).start()

    def arrived(kind, buffer):
        pltpu.make_async_copy(buffer, buffer, head_recv.at[kind]).wait()

    def sent(kind, buffer):
        part = buffer.at[0 : n_head - 1]
        pltpu.make_async_copy(part, part, head_send.at[kind]).wait()

    def lanes(ref, start, size):
        return ref.at[:, pl.ds(pl.multiple_of(start, LANES), size)]

    scatter(0, lambda to: lanes(b_ref, lax.div(to, per_group) * STATE, STATE), b_buf.at[head])
    scatter(1, lambda to: lanes(c_ref, lax.div(to, per_group) * STATE, STATE), c_buf.at[head])
    scatter(2, lambda to: lanes(dt_ref, lax.div(to, per_tile) * LANES, LANES), dt_buf.at[head])
    scatter(3, lambda to: lanes(x_ref, to * width, width), x_buf.at[head])
    scatter(4, lambda to: lanes(dy_ref, to * width, width), dy_buf.at[head])

    lower = triangle(length, True)
    upper = triangle(length, False)
    lane = lax.broadcasted_iota(jnp.int32, (length, LANES), 1)
    arrived(0, b_buf)
    arrived(1, c_buf)
    arrived(2, dt_buf)
    shift = lax.rem(LANES - lax.rem(head, per_tile) * heads_dev, LANES)
    dt = jnp.where(lane < heads_dev, pltpu.roll(flat(dt_buf), shift, 1), 0.0)
    rate = par_ref[6:7, 0:LANES]
    cumul = -rate * nn(jnp.where(lower, 1.0, 0.0).astype(BF16), dt.astype(BF16))
    grow = expand(jnp.exp(cumul), width)
    tail = expand(jnp.exp(cumul[length - 1 : length, :] - cumul), width)
    dt_wide = expand(dt, width)
    b32 = flat(b_buf)
    c32 = flat(c_buf)
    b16 = b32.astype(BF16)
    c16 = c32.astype(BF16)
    b_turned = b32.T.astype(BF16)
    c_turned = c32.T.astype(BF16)
    decay_own[...] = jnp.broadcast_to(grow[length - 1 : length, :], (8, width))
    decay_copy = remote(
        decay_own, decay_sib, (decay_sems.at[0], decay_sems.at[1]), sibling
    )
    decay_copy.start()
    arrived(3, x_buf)
    edge_copy = remote(
        x_buf.at[n_head - 1, tok_dev - 8 : tok_dev, :],
        edge,
        (edge_sems.at[0], edge_sems.at[1]),
        following,
    )
    edge_copy.start()
    arrived(4, dy_buf)
    dy = flat(dy_buf)
    dy16 = dy.astype(BF16)
    dy_grown = dy * grow
    pull = exact_by(nn, c_turned, dy_grown)

    edge_copy.wait()
    ext[0:8, :] = jnp.where(me > 0, edge[...].astype(F32), 0.0)
    conv, sig = convolve(flat(x_buf), par_ref, ext)
    activ = conv * sig
    slope = sig * (1.0 + conv * (1.0 - sig))
    source = activ * dt_wide
    state = exact_by(nn, b_turned, source * tail)
    first_core = core == 0
    other[...] = jnp.where(first_core, pull, state)
    mine[...] = jnp.where(first_core, state, pull)
    local_copy = remote(
        other, sib_local, (local_sems.at[0], local_sems.at[1]), sibling
    )
    local_copy.start()

    def within():
        turned = cumul.T
        gram = nt(c16, b16)
        gram_turned = nt(b16, c16)
        g_gram = jnp.zeros((length, length), F32)
        g_cumul = jnp.zeros((length, LANES), F32)
        for pair in range(width // LANES):
            at = slice(pair * LANES, (pair + 1) * LANES)
            src_hi, src_lo = split(source[:, at])
            halves = []
            for side in range(2):
                h = 2 * pair + side
                own = lane < HEAD_DIM if side == 0 else lane >= HEAD_DIM
                dy_own = jnp.where(own, dy[:, at], 0.0).astype(BF16)
                col = cumul[:, h : h + 1]
                row = turned[h : h + 1, :]
                decay = jnp.where(lower, jnp.exp(jnp.minimum(col - row, 0.0)), 0.0)
                inside = decay * (nt(dy_own, src_hi) + nt(dy_own, src_lo))
                g_gram = g_gram + inside
                g_cumul = g_cumul + jnp.where(
                    lane == h, jnp.sum(inside * gram, axis=1, keepdims=True), 0.0
                )
                mixing = gram_turned * jnp.where(
                    upper, jnp.exp(jnp.minimum(row - col, 0.0)), 0.0
                )
                halves.append(wide_by(nn, mixing, dy16[:, at]))
            inner[:, at] = jnp.where(lane < HEAD_DIM, halves[0], halves[1])
        gram_sum[...] = g_gram
        cumul_sum[...] = g_cumul

    late = place >= (chips + 1) // 2

    @pl.when(place == 0)
    def _():
        chain_in[...] = jnp.zeros_like(chain_in)

    decay_copy.wait()
    local_copy.wait()

    @pl.when(late)
    def _():
        within()

    def chain_copy(c):
        rows = pl.ds(pl.multiple_of(c * CHUNK, CHUNK), CHUNK)
        return remote(
            chain_out.at[rows, :],
            chain_in.at[rows, :],
            (chain_send.at[c], chain_recv.at[c]),
            ahead,
        )

    def sib_copy(c):
        rows = pl.ds(pl.multiple_of(c * CHUNK, CHUNK), CHUNK)
        return remote(
            sib_out.at[rows, :],
            sib_in.at[rows, :],
            (sib_send.at[c], sib_recv.at[c]),
            sibling,
        )

    def hop(c, _):
        rows = pl.ds(pl.multiple_of(c * CHUNK, CHUNK), CHUNK)

        @pl.when(place > 0)
        def _():
            chain_copy(c).wait_recv()

        here = decay_own[0:1, :] * chain_in[rows, :] + mine[rows, :]
        chain_out[rows, :] = decay_sib[0:1, :] * here + sib_local[rows, :]

        @pl.when(place < chips - 1)
        def _():
            chain_copy(c).start()

        sib_out[rows, :] = here
        sib_copy(c).start()
        return 0

    chunks = STATE // CHUNK
    lax.fori_loop(0, chunks, hop, 0)

    @pl.when(jnp.logical_not(late))
    def _():
        within()

    def drain(c, _):
        @pl.when(place < chips - 1)
        def _():
            chain_copy(c).wait_send()

        sib_copy(c).wait()
        return 0

    lax.fori_loop(0, chunks, drain, 0)

    state = jnp.where(first_core, chain_in[...], sib_in[...])
    pull = jnp.where(first_core, sib_in[...], chain_in[...])
    pulled = tail * exact_by(nn, b16, pull)
    g_source = inner[...] + pulled
    g_conv = (dt_wide * g_source + expand(par_ref[7:8, 0:LANES], width) * dy) * slope
    ext[0:length, :] = g_conv
    top_out[...] = g_conv[0:8, :]
    top_copy = remote(top_out, top_in, (top_sems.at[0], top_sems.at[1]), leading)
    top_copy.start()

    def by_token(value):
        return value.reshape(n_head, tok_dev, value.shape[1])

    g_gram = gram_sum[...]
    gb_buf[...] = by_token(
        wide_by(nn, g_gram.T, c16) + three(nt, source * tail, pull)
    )
    scatter(5, lambda to: gb_buf.at[to], gb_all.at[head])
    gc_buf[...] = by_token(wide_by(nn, g_gram, b16) + three(nt, dy_grown, state))
    scatter(6, lambda to: gc_buf.at[to], gc_all.at[head])

    top_copy.wait()
    ext[length : length + 8, :] = jnp.where(me < n_ctx - 1, top_in[...], 0.0)
    g_x = par_ref[3:4, :] * g_conv
    for k in range(CONV - 1):
        g_x = g_x + par_ref[k : k + 1, :] * ext[CONV - 1 - k : CONV - 1 - k + length, :]
    gx_buf[...] = by_token(g_x).astype(BF16)
    scatter(7, lambda to: gx_buf.at[to], lanes(gx_ref, head * width, width))

    direct = segments(activ * g_source)
    g_cumul = (
        cumul_sum[...] + segments(dy_grown * exact_by(nn, c16, state)) - dt * direct
    )
    carried = jnp.sum(source * pulled, axis=0, keepdims=True) + grow[
        length - 1 : length, :
    ] * jnp.sum(state * pull, axis=0, keepdims=True)
    carried = segments(jnp.broadcast_to(carried, (16, width)))[0:1, :]
    after = jnp.where(upper, 1.0, 0.0).astype(BF16)
    pieces = split(g_cumul, 3)
    later = nn(after, pieces[0]) + (nn(after, pieces[1]) + nn(after, pieces[2]))
    g_dt = direct - rate * (later + carried)
    merged = jnp.zeros((length, LANES), F32)
    for j, part in enumerate(split(g_dt, 3)):
        part = part.astype(F32)
        merged = merged + (pltpu.roll(part, j * heads_dev, 1) if j else part)
    gdt_buf[...] = by_token(merged).astype(BF16)
    scatter(8, lambda to: gdt_buf.at[to], gdt_all.at[head])

    for kind, buffer, result in ((5, gb_all, gb_ref), (6, gc_all, gc_ref)):
        arrived(kind, buffer)
        for g in range(GROUPS):
            summed = buffer[g * per_group]
            for j in range(1, per_group):
                summed = summed + buffer[g * per_group + j]
            result[:, g * STATE : (g + 1) * STATE] = summed.astype(BF16)
    arrived(8, gdt_all)
    own = lax.broadcasted_iota(jnp.int32, (tok_dev, LANES), 1) < heads_dev
    for tile in range(n_head // per_tile):
        summed = jnp.zeros((tok_dev, LANES), F32)
        for j in range(per_tile):
            value = gdt_all[tile * per_tile + j].astype(F32)
            value = (
                value
                + pltpu.roll(value, LANES - heads_dev, 1)
                + pltpu.roll(value, LANES - 2 * heads_dev, 1)
            )
            value = jnp.where(own, value, 0.0)
            summed = summed + (pltpu.roll(value, j * heads_dev, 1) if j else value)
        gdt_ref[:, tile * LANES : (tile + 1) * LANES] = summed
    arrived(7, gx_ref)
    for kind, buffer in enumerate(
        (b_buf, c_buf, dt_buf, x_buf, dy_buf, gb_buf, gc_buf, gx_buf, gdt_buf)
    ):
        sent(kind, buffer)


def shards(x_in, grad_y, b_in, c_in, dt, conv_weight, conv_bias, decay_rate, skip):
    n_head = lax.axis_size("head")
    n_ctx = lax.axis_size("ctx")
    per_group = n_head // GROUPS
    tok_dev = x_in.shape[0]
    heads_dev = decay_rate.shape[0]
    width = heads_dev * HEAD_DIM
    length = tok_dev * n_head

    whole = pltpu.VMEM((STATE, width), F32)
    small = pltpu.VMEM((8, width), F32)
    held = lambda size, kind: pltpu.VMEM((n_head, tok_dev, size), kind)
    pair = pltpu.SemaphoreType.DMA((2,))
    many = pltpu.SemaphoreType.DMA((STATE // CHUNK,))
    return pl.pallas_call(
        functools.partial(block_kernel, n_ctx, n_head),
        out_shape=(
            jax.ShapeDtypeStruct(x_in.shape, BF16),
            jax.ShapeDtypeStruct(b_in.shape, BF16),
            jax.ShapeDtypeStruct(c_in.shape, BF16),
            jax.ShapeDtypeStruct(dt.shape, F32),
        ),
        in_specs=[pl.BlockSpec(memory_space=pltpu.VMEM)] * 9,
        out_specs=[pl.BlockSpec(memory_space=pltpu.VMEM)] * 4,
        scratch_shapes=[
            held(width, BF16),
            held(width, BF16),
            held(STATE, BF16),
            held(STATE, BF16),
            held(LANES, BF16),
            held(width, BF16),
            held(STATE, F32),
            held(STATE, F32),
            held(LANES, BF16),
            held(STATE, F32),
            held(STATE, F32),
            held(LANES, BF16),
            small,
            pltpu.SemaphoreType.DMA((9,)),
            pltpu.SemaphoreType.DMA((9,)),
            pltpu.VMEM((length + 8, width), F32),
            pltpu.VMEM((8, width), BF16),
            small,
            small,
            whole,
            whole,
            whole,
            small,
            small,
            whole,
            whole,
            whole,
            whole,
            pltpu.VMEM((length, length), F32),
            pltpu.VMEM((length, LANES), F32),
            pltpu.VMEM((length, width), F32),
            pair,
            pair,
            pair,
            pair,
            many,
            many,
            many,
            many,
        ],
        compiler_params=pltpu.CompilerParams(
            vmem_limit_bytes=56 * 1024 * 1024, collective_id=0, has_side_effects=True
        ),
    )(
        x_in,
        grad_y,
        b_in,
        c_in,
        dt,
        conv_weight,
        conv_bias[None, :],
        decay_rate[None, :],
        skip[None, :],
    )


def solution(mesh):
    token = P(("ctx", "head"), None)
    in_specs = (token,) * 5 + (P(None, "head"), P("head"), P("head"), P("head"))
    return jax.shard_map(
        shards, mesh=mesh, in_specs=in_specs, out_specs=(token,) * 4, check_vma=False
    )
```
